128 devices in a mesh: fluid: 16 (over z, y), sub: 8 (over x, core).
Axes of the slice: x: 4, y: 4, z: 4, core: 2. Of those that a mesh axis runs over, the one named last changes fastest.
Arguments:
- positions: float32 [3, 262144], P(None, ('fluid', 'sub')), may hold values from 0 to 1
- particle_temp: float32 [262144], P(('fluid', 'sub')), may hold values from -6 to 6
- pair_list: int32 [32768, 2], P(('fluid', 'sub')), may hold values from 0 to 31, as said below
- pair_count: int32 [128], P(('fluid', 'sub')), may hold values from 16 to 256, as said below
- ghost_particle: int32 [262144], P(('fluid', 'sub')), may hold values from 0 to 2047
- ghost_owner: int32 [262144, 1], P(('fluid', 'sub')), may hold values from 0 to 127; in each aligned block of 2048 rows (0 to 2047, 2048 to 4095, ...) at most 32 rows name the same one
- ghost_cell: int32 [262144], P(('fluid', 'sub')), may hold values from 0 to 32767
- wall_seen: float32 [262144], P(('fluid', 'sub')), may hold values from -6 to 6
- solid_temp: float32 [32, 2048, 2048], P(None, ('fluid', 'sub')), may hold values from -6 to 6
- conduct: float32 [32, 2048, 2048], P(None, ('fluid', 'sub')), may hold values from 0.03 to 0.16
Outputs:
- particle_out: float32 [262144], P(('fluid', 'sub'))
- solid_out: float32 [32, 2048, 2048], P(None, ('fluid', 'sub'))
- ghost_temp: float32 [262144], P(('fluid', 'sub'))
The draws below stay inside these ranges and needn't reach their ends.
Inputs may be any that keep to these rules, and one draw needn't show every extreme that they name: `pair_list`: column 0 names one of the device's own tiles; column 1 names own tile t below 16, or tile t - 16 of the next device along sub, cyclically. `pair_count`: rows of a device's block beyond its count are not used; some device uses all 256. `ghost_owner`: among the 2048 ghosts of one device, at most 32 name the same owner.
All inputs are finite; a program needn't handle non-finite values.
Results may differ from the reference program's by a relative error of at most 0.0003.
Values sent between devices are 32-bit elements; how exact they have to be, the bound alone decides.
A program may use at most 128 MiB of HBM per device.

```python
import math
import jax
import jax.numpy as jnp
import numpy as np
from jax import lax

TILE = 128
TILES = 16
PAIRS = 256
GHOST_DEV = 2048
SX = 16
NZS = 2048
DEPTH = 32
SUBSTEPS = 6
DEVICES_ALL = 128
CAP = 32
PARTICLES = 262144
PAIR_ROWS = 32768
GHOSTS = 262144
NXS = 2048
N_FLUID = 16
N_SUB = 8


def draw_pair_list(key, part):
    first_key, second_key = jax.random.split(jax.random.fold_in(key, 11))
    first_tile = jax.random.randint(first_key, (PAIR_ROWS,), 0, TILES)
    second_tile = jax.random.randint(second_key, (PAIR_ROWS,), 0, 2 * TILES)
    return jnp.stack([first_tile, second_tile], axis=1).astype(jnp.int32)


def draw_pair_count(key, part):
    count_key, chosen_key = jax.random.split(jax.random.fold_in(key, 23))
    devices = PAIR_ROWS // PAIRS
    counts = jax.random.randint(count_key, (devices,), PAIRS // 16, PAIRS + 1)
    chosen = jax.random.randint(chosen_key, (), 0, devices)
    return counts.at[chosen].set(PAIRS).astype(jnp.int32)


def set_ends(array, rng, low, largest):
    index_at = [jax.random.randint(jax.random.fold_in(rng, axis), (), 0, length) for axis, length in enumerate(array.shape)]
    main_axis = array.shape.index(max(array.shape))
    neighbour = index_at[:main_axis] + [(index_at[main_axis] + 1) % array.shape[main_axis]] + index_at[main_axis + 1:]
    return array.at[tuple(index_at)].set(low).at[tuple(neighbour)].set(largest)


def steps_of(own_key, dims, cuts, least, high):
    def one(dim, blocks):
        heights = jax.random.uniform(jax.random.fold_in(jax.random.fold_in(own_key, 6), dim), (blocks,), jnp.float32, least / len(cuts), high / len(cuts))
        return jnp.repeat(jnp.exp(heights), dims[dim] // blocks).reshape((-1,) + (1,) * (len(dims) - dim - 1))

    level = one(*cuts[0])
    for cut in cuts[1:]:
        level = level * one(*cut)
    return level


def deal_out(rng, own, number, rows, count, top, bound, lean):
    ranking = jax.random.permutation(rng, count)
    packed, common = load_shares(count, rows * top, bound, lean, True), load_shares(count, rows * top, bound, lean, False)
    places = jnp.arange(count)

    def named(lengths, offset_by):
        used = int((lengths > 0).sum())
        fixed = max(1, used // 4)
        passed = fixed + (places - fixed + offset_by * (used - fixed)) % max(1, count - fixed)
        return jnp.zeros((count,), jnp.int32).at[ranking[jnp.where(places < fixed, places, passed)]].set(jnp.asarray(lengths, jnp.int32))

    lengths = jnp.where(number % 4 == 0, named(packed, number // 4), named(common, number - number // 4 - 1))
    mixed = jax.random.permutation(jax.random.fold_in(own, 3), count)
    donor, sink = mixed[0:count // 2 * 2:2], mixed[1:count // 2 * 2:2]
    slack = jnp.minimum(lengths[donor] - 1, bound - lengths[sink]) // 2
    slack = jnp.where((donor == ranking[0]) | (sink == ranking[0]) | (lengths[sink] == 0), 0, jnp.maximum(slack, 0))
    passed = jax.random.randint(jax.random.fold_in(own, 4), (count // 2,), 0, 1 << 20) % (slack + 1)
    lengths = lengths.at[donor].add(-passed).at[sink].add(passed)
    labels = jnp.searchsorted(jnp.cumsum(lengths), jnp.arange(rows * top), side="right").astype(jnp.int32)
    grid = labels.reshape(top, rows).T
    grid = grid[jax.random.permutation(jax.random.fold_in(own, 1), rows)]
    offset_by = jax.random.randint(jax.random.fold_in(own, 2), (rows, 1), 0, top)
    return jnp.take_along_axis(grid, (jnp.arange(top)[None, :] + offset_by) % top, axis=1)


def load_shares(count, total, reach, slope, full):
    weights = [(1 << 20) // math.isqrt(grade ** slope) + 1 for grade in range(1, count + 1)]
    largest = reach if full else min(reach, max(-(-total // count), total * weights[0] // sum(weights)))
    least = 1 if total - largest >= count - 1 else 0
    given, surplus = [largest] + [least] * (count - 1), total - largest - least * (count - 1)
    while surplus > 0:
        free = [i for i in range(1, count) if given[i] < largest] or [i for i in range(1, count) if given[i] < reach]
        mass, budget = sum([weights[i] for i in free]), surplus
        for i in free:
            extra = min(reach - given[i], max(1, budget * weights[i] // mass), surplus)
            given[i] = given[i] + extra
            surplus = surplus - extra
    return np.array(given)


def scatter_about(own_key, dims, scale, limit, cuts=(), held_as=jnp.bfloat16):
    values = scale * jax.random.normal(own_key, dims, jnp.float32)
    if cuts:
        values = values * steps_of(own_key, dims, cuts, -0.22, 0.18)
    return jnp.clip(values, -limit, limit).astype(held_as)


def setup_inputs(seed: int = 0) -> dict:
    keys = jax.random.split(jax.random.key(seed), 11)
    positions = jnp.clip(1.0 * jax.random.uniform(keys[0], (3, PARTICLES), jnp.float32) ** steps_of(keys[0], (3, PARTICLES), ((1, 128),), -0.2, 0.2), 0.0, 1.0)
    particle_temp = scatter_about(keys[1], (PARTICLES,), 1.0, 6.0, ((0, 128),), jnp.float32)
    pair_list = draw_pair_list(jax.random.fold_in(keys[10], 71), 0)
    pair_count = draw_pair_count(jax.random.fold_in(keys[10], 71), 0)
    ghost_particle = set_ends(jax.random.randint(keys[4], (GHOSTS,), 0, TILES * TILE), jax.random.fold_in(keys[4], 1), 0, (TILES * TILE) - 1).astype(jnp.int32)
    ghost_owner_keys = jax.random.split(jax.random.fold_in(keys[5], 1), GHOSTS // GHOST_DEV)
    ghost_owner_turns = jax.random.permutation(jax.random.fold_in(keys[5], 3), GHOSTS // GHOST_DEV)
    ghost_owner = jax.vmap(lambda own, number: deal_out(jax.random.fold_in(keys[5], 2), own, number, GHOST_DEV, DEVICES_ALL, 1, CAP, 2))(ghost_owner_keys, ghost_owner_turns).reshape((GHOSTS, 1))
    ghost_cell = set_ends(jax.random.randint(keys[6], (GHOSTS,), 0, SX * NZS), jax.random.fold_in(keys[6], 1), 0, (SX * NZS) - 1).astype(jnp.int32)
    wall_seen = scatter_about(keys[7], (GHOSTS,), 1.0, 6.0, ((0, 128),), jnp.float32)
    solid_temp = scatter_about(keys[8], (DEPTH, NXS, NZS), 1.0, 6.0, ((1, 128),), jnp.float32)
    conduct = jnp.clip(jnp.exp(math.log(0.16) - 1.6739764 * jax.random.uniform(keys[9], (DEPTH, NXS, NZS), jnp.float32) ** steps_of(keys[9], (DEPTH, NXS, NZS), ((1, 128),), -0.2, 0.2)), 0.03, 0.16)
    return dict(positions=positions, particle_temp=particle_temp, pair_list=pair_list, pair_count=pair_count, ghost_particle=ghost_particle, ghost_owner=ghost_owner, ghost_cell=ghost_cell, wall_seen=wall_seen, solid_temp=solid_temp, conduct=conduct)


heat_rate = 0.004
wall_heat = 0.5


def tile_heat(own_pos, own_temp, near_pos, near_temp, pairs, live_count, blocks):
    all_pos = jnp.concatenate([own_pos, near_pos], axis=1)
    all_temp = jnp.concatenate([own_temp, near_temp], axis=0)
    block_rows = 16

    def pair_block(number, accrued):
        pair_rows = lax.dynamic_slice_in_dim(pairs, number * block_rows, block_rows, 0)
        first_tile = pair_rows[:, 0]
        second_tile = pair_rows[:, 1]
        live_rows = (number * block_rows + jnp.arange(block_rows, dtype=jnp.int32)) < live_count
        left_pos = all_pos[:, first_tile, :]
        right_pos = all_pos[:, second_tile, :]
        distance = jnp.zeros((block_rows, left_pos.shape[2], right_pos.shape[2]), jnp.float32)
        for component in range(3):
            offset = left_pos[component][:, :, None] - right_pos[component][:, None, :]
            distance = distance + offset * offset
        kernel = jnp.square(jnp.maximum(0.0, 1.0 - distance))
        gained = jnp.sum(kernel * (all_temp[second_tile][:, None, :] - all_temp[first_tile][:, :, None]), axis=2)
        gained = jnp.where(live_rows[:, None], gained, 0.0)
        return accrued.at[first_tile].add(gained)

    accrued = lax.fori_loop(0, blocks, pair_block, jnp.zeros(own_temp.shape, jnp.float32))
    return own_temp + heat_rate * accrued


def solid_step(padded, coef, source):
    center = padded[1:-1, 1:-1, 1:-1]
    beside = padded[2:, 1:-1, 1:-1] + padded[:-2, 1:-1, 1:-1]
    beside = beside + padded[1:-1, 2:, 1:-1] + padded[1:-1, :-2, 1:-1]
    beside = beside + padded[1:-1, 1:-1, 2:] + padded[1:-1, 1:-1, :-2]
    result = center + coef * (beside - 6.0 * center)
    return result.at[0].add(source)


def reference(positions, particle_temp, pair_list, pair_count, ghost_particle, ghost_owner, ghost_cell, wall_seen, solid_temp, conduct):
    devices = N_FLUID * N_SUB
    per_device = TILES * TILE
    pos_tiles = positions.reshape(3, N_FLUID, N_SUB, TILES, TILE)
    temp_tiles = particle_temp.reshape(N_FLUID, N_SUB, TILES, TILE)
    near_pos = jnp.roll(pos_tiles, -1, axis=2)
    near_temp = jnp.roll(temp_tiles, -1, axis=1)
    own_pos = jnp.moveaxis(pos_tiles.reshape(3, devices, TILES, TILE), 1, 0)
    near_pos = jnp.moveaxis(near_pos.reshape(3, devices, TILES, TILE), 1, 0)
    own_temp = temp_tiles.reshape(devices, TILES, TILE)
    near_temp = near_temp.reshape(devices, TILES, TILE)
    pairs = pair_list.reshape(devices, PAIRS, 2)

    def one_device(items):
        return tile_heat(items[0], items[1], items[2], items[3], items[4], items[5], PAIRS // 16)

    heated = lax.map(one_device, (own_pos, own_temp, near_pos, near_temp, pairs, pair_count))
    particle_out = heated.reshape(-1)
    owner = ghost_owner[:, 0]
    source_index = ghost_particle + (jnp.arange(GHOSTS, dtype=jnp.int32) // GHOST_DEV) * per_device
    flux = wall_heat * (particle_out[source_index] - wall_seen)
    wall_index = owner * (SX * NZS) + ghost_cell
    surface = jnp.zeros((NXS * NZS,), jnp.float32).at[wall_index].add(flux).reshape(NXS, NZS)
    source = surface / SUBSTEPS
    temp = solid_temp
    for turn in range(SUBSTEPS):
        temp = solid_step(jnp.pad(temp, 1), conduct, source)
    ghost_temp = temp[0].reshape(-1)[wall_index]
    return particle_out, temp, ghost_temp
```

```python
import functools
import jax
import jax.numpy as jnp
from jax import lax
from jax.experimental import pallas as pl
from jax.experimental.pallas import tpu as pltpu
from jax.sharding import PartitionSpec as P

F32, BF16, I32 = jnp.float32, jnp.bfloat16, jnp.int32
TILE = 128
SUBSTEPS = 6
SLOTS = 32
HEAT_RATE = 0.004
WALL_HEAT = 0.5
UNROLL = 8
AXES = ("fluid", "sub")
VMEM_SPEC = pl.BlockSpec(memory_space=pltpu.VMEM)
SMEM_SPEC = pl.BlockSpec(memory_space=pltpu.SMEM)
ANY_SPEC = pl.BlockSpec(memory_space=pl.ANY)


def split3(x):
    high = x.astype(BF16).astype(F32)
    rest = x - high
    mid = rest.astype(BF16).astype(F32)
    return high, mid, rest - mid


def row_of(ref):
    return jnp.concatenate([ref[t : t + 1, :] for t in range(ref.shape[0])], axis=1)


def onehot(rows, codes, dtype=BF16):
    shape = (rows, codes.shape[1])
    hit = lax.broadcasted_iota(I32, shape, 0) == jnp.broadcast_to(codes, shape)
    return jnp.where(hit, 1.0, 0.0).astype(dtype)


def dot_nn(a, b):
    return lax.dot_general(a, b, (((1,), (0,)), ((), ())), preferred_element_type=F32)


def dot_nt(a, b):
    return lax.dot_general(a, b, (((1,), (1,)), ((), ())), preferred_element_type=F32)


def put_features(pos, temp_row, left, right):
    wide = pos.shape[1]
    moved = pos - 0.5
    high, mid, low = split3(moved)
    squares = jnp.sum(moved * moved, axis=0, keepdims=True)
    one = jnp.ones((3, wide), F32)
    minus = split3(-squares)
    temps = split3(temp_row)
    for place, part in enumerate((high, high, mid, mid, high, low)):
        left[3 * place : 3 * place + 3, :] = part
    left[18:21, :] = one
    for k in range(3):
        left[21 + k : 22 + k, :] = minus[k]
        left[24 + k : 25 + k, :] = temps[k]
    left[27:30, :] = one
    left[30:32, :] = jnp.zeros((2, wide), F32)
    if right is None:
        return
    base = split3(1.0 - squares)
    for place, part in enumerate((high, mid, high, mid, low, high)):
        right[3 * place : 3 * place + 3, :] = 2.0 * part
    right[21:24, :] = one
    right[24:27, :] = one
    for k in range(3):
        right[18 + k : 19 + k, :] = base[k]
        right[27 + k : 28 + k, :] = -temps[k]
    right[30:32, :] = jnp.zeros((2, wide), F32)


def pair_heat(own_pos, own_temp, near_pos, near_temp, codes, count, left, right, lefts, rights, acc):
    tiles = own_temp.shape[0]
    for base, pos, temp, second in ((0, own_pos, own_temp, right), (tiles, near_pos, near_temp, None)):
        put_features(pos[...], row_of(temp), left, second)
        for t in range(tiles):
            block = left[:, t * TILE : (t + 1) * TILE]
            lefts[base + t] = block.T.astype(BF16)
    for t in range(tiles):
        block = right[:, t * TILE : (t + 1) * TILE]
        upper = lax.broadcasted_iota(I32, block.shape, 0) < 24
        rights[t, :, 0:TILE] = jnp.where(upper, block, 0.0).astype(BF16)
        rights[t, :, TILE : 2 * TILE] = jnp.where(upper, 0.0, block).astype(BF16)
    acc[...] = jnp.zeros(acc.shape, F32)
    live = count[0]

    def body(group, _):
        for k in range(UNROLL):
            number = group * UNROLL + k
            code = codes[number]
            first = lax.shift_right_logical(code, 5) & (tiles - 1)
            second = code & (2 * tiles - 1)
            both = dot_nn(lefts[second], rights[first])
            near = jnp.maximum(both[:, :TILE], 0.0)
            gained = near * near * both[:, TILE:]
            gained = jnp.sum(gained.reshape(TILE // 8, 8, TILE), axis=0)
            acc[first] += jnp.where(number < live, gained, 0.0)
        return 0

    lax.fori_loop(0, (live + UNROLL - 1) // UNROLL, body, 0)
    return own_temp[...] + HEAT_RATE * jnp.sum(acc[...], axis=1)


def ranks(owners, devices):
    row = lax.broadcasted_iota(I32, (TILE, 2 * TILE), 0)
    col = lax.broadcasted_iota(I32, (TILE, 2 * TILE), 1)
    before = jnp.where((row < col) | (col >= TILE), 1.0, 0.0).astype(BF16)
    so_far = jnp.zeros((devices, TILE), F32)
    out = []
    for t in range(owners.shape[1] // TILE):
        mine = owners[:, t * TILE : (t + 1) * TILE]
        counted = dot_nn(mine, before)
        out.append(jnp.sum(mine.astype(F32) * (counted[:, :TILE] + so_far), axis=0, keepdims=True))
        so_far = so_far + counted[:, TILE:]
    return jnp.concatenate(out, axis=1)


def particles_kernel(codes, count, own_pos, own_temp, near_pos, near_temp, which, owner, cell, seen,
                     heated, send, rank_out, left, right, lefts, rights, acc):
    out = pair_heat(own_pos, own_temp, near_pos, near_temp, codes, count, left, right, lefts, rights, acc)
    heated[...] = out
    devices = send.shape[0]
    owners = onehot(devices, row_of(owner))
    rank = ranks(owners, devices)
    for t in range(rank_out.shape[0]):
        rank_out[t : t + 1, :] = rank[:, t * TILE : (t + 1) * TILE].astype(I32)
    tiles = out.shape[0]
    parts = jnp.concatenate(split3(out), axis=0).T.astype(BF16)
    which_row = row_of(which)
    high = onehot(tiles, lax.shift_right_logical(which_row, 7))
    picked = dot_nn(parts, jnp.concatenate([high] * 3, axis=0))
    low = jnp.broadcast_to(which_row & (TILE - 1), picked.shape)
    hit = lax.broadcasted_iota(I32, picked.shape, 0) == low
    value = jnp.sum(jnp.where(hit, picked, 0.0), axis=0, keepdims=True)
    flux = WALL_HEAT * (value - row_of(seen))
    slot = onehot(SLOTS, rank.astype(I32), F32)
    cell_row = row_of(cell)
    cell_high = (cell_row & ~255).astype(F32)
    cell_low = (cell_row & 255).astype(F32)
    fluxes = split3(flux)
    total = jnp.zeros((devices, 2 * SLOTS), F32)
    for f, c in zip(fluxes, (cell_high, cell_low, jnp.zeros_like(cell_low))):
        rows = jnp.concatenate([slot * f, slot * c], axis=0).astype(BF16)
        total = total + dot_nt(owners, rows)
    send[...] = jnp.zeros(send.shape, F32)
    send[:, 0 : 2 * SLOTS] = total


def call_particles(codes, count, own_pos, own_temp, near_pos, near_temp, which, owner, cell, seen, devices):
    tiles = own_temp.shape[0]
    wide = own_pos.shape[1]
    return pl.pallas_call(
        particles_kernel,
        out_shape=(
            jax.ShapeDtypeStruct(own_temp.shape, F32),
            jax.ShapeDtypeStruct((devices, TILE), F32),
            jax.ShapeDtypeStruct(owner.shape, I32),
        ),
        in_specs=[SMEM_SPEC] * 2 + [VMEM_SPEC] * 8,
        out_specs=(VMEM_SPEC,) * 3,
        scratch_shapes=[
            pltpu.VMEM((32, wide), F32),
            pltpu.VMEM((32, wide), F32),
            pltpu.VMEM((2 * tiles, TILE, 32), BF16),
            pltpu.VMEM((tiles, 32, 2 * TILE), BF16),
            pltpu.VMEM((tiles, 8, TILE), F32),
        ],
        name="particles",
    )(codes, count, own_pos, own_temp, near_pos, near_temp, which, owner, cell, seen)


def spread_kernel(recv, surface, hot, lows):
    turned = recv[...].T
    slots, sources = SLOTS, recv.shape[0]
    for s in range(slots):
        code = turned[slots + s : slots + s + 1, :].astype(I32)
        flux = turned[s : s + 1, :]
        at = pl.ds(s * sources, sources)
        hot[:, at] = onehot(hot.shape[0], lax.shift_right_logical(code, 7))
        low = onehot(TILE, code & (TILE - 1), F32)
        for k, part in enumerate(split3(flux)):
            lows[k, :, at] = (low * part).astype(BF16)
    total = dot_nt(hot[...], lows[0])
    total = total + dot_nt(hot[...], lows[1])
    surface[...] = total + dot_nt(hot[...], lows[2])


def call_spread(recv, cells):
    rows = cells // TILE
    slots = recv.shape[0] * SLOTS
    return pl.pallas_call(
        spread_kernel,
        out_shape=jax.ShapeDtypeStruct((rows, TILE), F32),
        in_specs=[VMEM_SPEC],
        out_specs=VMEM_SPEC,
        scratch_shapes=[pltpu.VMEM((rows, slots), BF16), pltpu.VMEM((3, TILE, slots), BF16)],
        name="spread",
    )(recv)


def pick_kernel(surface, recv, values):
    turned = recv[...].T
    rows = surface.shape[0]
    flat = surface[...]
    parts = [p.astype(BF16) for p in split3(jnp.concatenate([flat[k : k + TILE, :].T for k in range(0, rows, TILE)], axis=1))]
    sources = recv.shape[0]
    out = []
    for s in range(SLOTS):
        code = turned[SLOTS + s : SLOTS + s + 1, :].astype(I32)
        high = onehot(rows, lax.shift_right_logical(code, 7))
        found = dot_nn(parts[0], high) + dot_nn(parts[1], high) + dot_nn(parts[2], high)
        low = lax.broadcasted_iota(I32, found.shape, 0) == jnp.broadcast_to(code & (TILE - 1), found.shape)
        out.append(jnp.sum(jnp.where(low, found, 0.0), axis=0, keepdims=True))
    out.append(jnp.zeros((TILE - SLOTS, sources), F32))
    values[...] = jnp.concatenate(out, axis=0).T


def call_pick(surface, recv):
    return pl.pallas_call(
        pick_kernel,
        out_shape=jax.ShapeDtypeStruct(recv.shape, F32),
        in_specs=[VMEM_SPEC] * 2,
        out_specs=VMEM_SPEC,
        name="pick",
    )(surface, recv)


def unpack_kernel(values, owner, rank, out):
    devices = values.shape[0]
    owners = onehot(devices, row_of(owner))
    turned = values[...].T[0:SLOTS, :]
    parts = jnp.concatenate(split3(turned), axis=0).astype(BF16)
    found = dot_nn(parts, owners)
    slot = onehot(SLOTS, row_of(rank), F32)
    total = found[0:SLOTS] + found[SLOTS : 2 * SLOTS] + found[2 * SLOTS :]
    ghost = jnp.sum(total * slot, axis=0, keepdims=True)
    for t in range(out.shape[0]):
        out[t : t + 1, :] = ghost[:, t * TILE : (t + 1) * TILE]


def call_unpack(values, owner, rank):
    return pl.pallas_call(
        unpack_kernel,
        out_shape=jax.ShapeDtypeStruct(owner.shape, F32),
        in_specs=[VMEM_SPEC] * 3,
        out_specs=VMEM_SPEC,
        name="unpack",
    )(values, owner, rank)


MESH = pl.DeviceIdType.MESH


def where_is(index, subs):
    return (index // subs, index % subs)


def exchange_kernel(devices, subs, send, recv, send_sem, recv_sem, own_sem):
    me = lax.axis_index(AXES[0]) * subs + lax.axis_index(AXES[1])
    barrier = pltpu.get_barrier_semaphore()

    def greet(k, _):
        to = lax.rem(me + k, devices)
        pl.semaphore_signal(barrier, inc=1, device_id=where_is(to, subs), device_id_type=MESH)
        return 0

    lax.fori_loop(1, devices, greet, 0)
    own = pltpu.make_async_copy(send.at[pl.ds(me, 1)], recv.at[pl.ds(me, 1)], own_sem)
    own.start()
    pl.semaphore_wait(barrier, devices - 1)

    def push(k, _):
        to = lax.rem(me + k, devices)
        pltpu.make_async_remote_copy(
            src_ref=send.at[pl.ds(to, 1)], dst_ref=recv.at[pl.ds(me, 1)], send_sem=send_sem, recv_sem=recv_sem,
            device_id=where_is(to, subs), device_id_type=MESH).start()
        return 0

    lax.fori_loop(1, devices, push, 0)
    own.wait()
    every = pltpu.make_async_remote_copy(
        src_ref=send.at[pl.ds(0, devices - 1)], dst_ref=recv.at[pl.ds(0, devices - 1)], send_sem=send_sem,
        recv_sem=recv_sem, device_id=where_is(me, subs), device_id_type=MESH)
    every.wait_recv()
    every.wait_send()


def call_exchange(send, devices, subs, number):
    return pl.pallas_call(
        functools.partial(exchange_kernel, devices, subs),
        out_shape=jax.ShapeDtypeStruct(send.shape, F32),
        in_specs=[VMEM_SPEC],
        out_specs=VMEM_SPEC,
        scratch_shapes=[pltpu.SemaphoreType.DMA] * 3,
        compiler_params=pltpu.CompilerParams(collective_id=number, has_side_effects=True),
        name="exchange",
    )(send)


PADZ = 32


def relayout_in(stage, dst, layers, rows, pitch, first, offset):
    blocks = stage.shape[2] // TILE

    def layer(l, _):
        base = (l + first) * (rows * pitch) + offset
        for xt in range(rows // 8):
            for zt in range(blocks):
                part = stage[l, xt * 8 : xt * 8 + 8, zt * TILE : (zt + 1) * TILE]
                dst[pl.ds(base + xt * 8 * pitch + zt, 8, stride=pitch), :] = part
        return 0

    lax.fori_loop(0, layers, layer, 0)


def solid_kernel(devices, subs, remote, temp, coef, surface, out, top_out,
                 stage, coef_stage, cur, nxt, coefs, sends, halos, load_sem, out_sem, send_sem, recv_sem):
    layers, rows, span = temp.shape
    blocks = span // TILE
    me = lax.axis_index(AXES[0]) * subs + lax.axis_index(AXES[1]) if remote else 5
    loads = [pltpu.make_async_copy(temp, stage, load_sem.at[0]), pltpu.make_async_copy(coef, coef_stage, load_sem.at[1])]
    for load in loads:
        load.start()
    if remote:
        barrier = pltpu.get_barrier_semaphore()

        for by in (1, devices - 1):
            pl.semaphore_signal(barrier, inc=1, device_id=where_is(lax.rem(me + by, devices), subs), device_id_type=MESH)

    def clear(l, _):
        for x in range(rows):
            base = pl.multiple_of((l * rows + x) * PADZ, 8)
            for buf in (cur, nxt):
                buf[pl.ds(base, 8), :] = jnp.zeros((8, TILE), F32)
                buf[pl.ds(base + 24, 8), :] = jnp.zeros((8, TILE), F32)
        return 0

    lax.fori_loop(0, layers + 2, clear, 0)
    for l in (0, layers + 1):
        for buf in (cur, nxt):
            buf[l * rows * PADZ : (l + 1) * rows * PADZ, :] = jnp.zeros((rows * PADZ, TILE), F32)

    for side, edge in ((0, 0), (1, devices - 1)):
        @pl.when(me == edge)
        def _():
            halos[:, side] = jnp.zeros((SUBSTEPS,) + halos.shape[2:], F32)

    def copies(k):
        return [pltpu.make_async_remote_copy(
            src_ref=sends.at[k, side], dst_ref=halos.at[k, 1 - side], send_sem=send_sem.at[k, side],
            recv_sem=recv_sem.at[k, 1 - side], device_id=where_is(me - 1 if side == 0 else me + 1, subs),
            device_id_type=MESH) for side in (0, 1)]

    has = (me > 0, me < devices - 1)

    def launch(k):
        if remote:
            for side in (0, 1):
                @pl.when(has[side])
                def _():
                    copies(k)[side].start()

    def arrive(k):
        if remote:
            for side in (0, 1):
                @pl.when(has[side])
                def _():
                    copies(k)[1 - side].wait_recv()

    def drain(k):
        if remote:
            for side in (0, 1):
                @pl.when(has[side])
                def _():
                    copies(k)[side].wait_send()

    loads[0].wait()
    relayout_in(stage, cur, layers, rows, PADZ, 1, 8)

    def edges(l, _):
        for side, x in ((0, 0), (1, rows - 1)):
            base = pl.multiple_of(((l + 1) * rows + x) * PADZ + 8, 8)
            sends[0, side, l] = cur[pl.ds(base, blocks), :]
        return 0

    lax.fori_loop(0, layers, edges, 0)
    if remote:
        pl.semaphore_wait(barrier, 2)
    launch(0)
    loads[1].wait()
    relayout_in(coef_stage, coefs, layers, rows, blocks, 0, 0)

    lane = lax.broadcasted_iota(I32, (blocks, TILE), 1)
    first_lane, last_lane = lane == 0, lane == TILE - 1

    def advance(k, src, dst, chosen):
        def layer(l, _):
            zero = jnp.where(l == 0, 1.0 / SUBSTEPS, 0.0)

            def at(step, x, shift=0):
                start = (l + 1 + step) * (rows * PADZ) + (x * PADZ + 8 + shift)
                return src[pl.ds(start, blocks), :]

            for x in chosen:
                center = at(0, x)
                after = pltpu.roll(jnp.where(first_lane, at(0, x, 1), center), TILE - 1, 1)
                before = pltpu.roll(jnp.where(last_lane, at(0, x, -1), center), 1, 1)
                above = halos[k, 0, l] if x == 0 else at(0, x - 1)
                below = halos[k, 1, l] if x == rows - 1 else at(0, x + 1)
                beside = (at(-1, x) + at(1, x)) + (above + below) + (after + before)
                c = coefs[pl.ds(pl.multiple_of(l * (rows * blocks) + x * blocks, 8), blocks), :]
                value = center + c * (beside - 6.0 * center)
                value = value + zero * surface[x * blocks : (x + 1) * blocks, :]
                base = (l + 1) * (rows * PADZ) + (x * PADZ + 8)
                dst[pl.ds(pl.multiple_of(base, 8), blocks), :] = value
                if k + 1 < SUBSTEPS and x in (0, rows - 1):
                    sends[k + 1, 0 if x == 0 else 1, l] = value
            return 0

        lax.fori_loop(0, layers, layer, 0)

    for k in range(SUBSTEPS):
        src, dst = (cur, nxt) if k % 2 == 0 else (nxt, cur)
        arrive(k)
        advance(k, src, dst, (0, rows - 1))
        if k + 1 < SUBSTEPS:
            launch(k + 1)
        advance(k, src, dst, tuple(range(1, rows - 1)))

    final = cur if SUBSTEPS % 2 == 0 else nxt

    def back(l, _):
        base = (l + 1) * (rows * PADZ) + 8
        for xt in range(rows // 8):
            for zt in range(blocks):
                stage[l, xt * 8 : xt * 8 + 8, zt * TILE : (zt + 1) * TILE] = final[pl.ds(base + xt * 8 * PADZ + zt, 8, stride=PADZ), :]
        return 0

    lax.fori_loop(0, layers, back, 0)
    store = pltpu.make_async_copy(stage, out, out_sem)
    store.start()
    for x in range(rows):
        base = rows * PADZ + x * PADZ + 8
        top_out[x * blocks : (x + 1) * blocks, :] = final[base : base + blocks, :]
    for k in range(SUBSTEPS):
        drain(k)
    store.wait()


def call_solid(temp, coef, surface, devices, subs, number, remote=True):
    layers, rows, span = temp.shape
    blocks = span // TILE
    return pl.pallas_call(
        functools.partial(solid_kernel, devices, subs, remote),
        out_shape=(jax.ShapeDtypeStruct(temp.shape, F32), jax.ShapeDtypeStruct(surface.shape, F32)),
        in_specs=[ANY_SPEC, ANY_SPEC, VMEM_SPEC],
        out_specs=(ANY_SPEC, VMEM_SPEC),
        scratch_shapes=[
            pltpu.VMEM(temp.shape, F32),
            pltpu.VMEM(temp.shape, F32),
            pltpu.VMEM(((layers + 2) * rows * PADZ, TILE), F32),
            pltpu.VMEM(((layers + 2) * rows * PADZ, TILE), F32),
            pltpu.VMEM((layers * rows * blocks, TILE), F32),
            pltpu.VMEM((SUBSTEPS, 2, layers, blocks, TILE), F32),
            pltpu.VMEM((SUBSTEPS, 2, layers, blocks, TILE), F32),
            pltpu.SemaphoreType.DMA((2,)),
            pltpu.SemaphoreType.DMA,
            pltpu.SemaphoreType.DMA((SUBSTEPS, 2)),
            pltpu.SemaphoreType.DMA((SUBSTEPS, 2)),
        ],
        compiler_params=pltpu.CompilerParams(
            **(dict(collective_id=number) if remote else {}), has_side_effects=True, vmem_limit_bytes=60 << 20),
        name="solid",
    )(temp, coef, surface)


def from_behind(value, axis, by):
    length = lax.axis_size(axis)
    return lax.ppermute(value, axis, [(i, (i + by) % length) for i in range(length)])


def on_device(positions, particle_temp, pair_list, pair_count, ghost_particle, ghost_owner, ghost_cell,
              wall_seen, solid_temp, conduct):
    devices = lax.axis_size(AXES[0]) * lax.axis_size(AXES[1])
    subs = lax.axis_size(AXES[1])
    own_temp = particle_temp.reshape(-1, TILE)
    near_pos, near_temp = from_behind((positions, own_temp), AXES[1], -1)
    codes = pair_list[:, 0] * 32 + pair_list[:, 1]
    owner = ghost_owner.reshape(-1, TILE)
    heated, send, rank = call_particles(
        codes, pair_count, positions, own_temp, near_pos, near_temp, ghost_particle.reshape(-1, TILE),
        owner, ghost_cell.reshape(-1, TILE), wall_seen.reshape(-1, TILE), devices)
    recv = call_exchange(send, devices, subs, 0)
    surface = call_spread(recv, solid_temp.shape[1] * solid_temp.shape[2])
    temp, top = call_solid(solid_temp, conduct, surface, devices, subs, 1)
    values = call_pick(top, recv)
    back = call_exchange(values, devices, subs, 2)
    ghost = call_unpack(back, owner, rank)
    return heated.reshape(-1), temp, ghost.reshape(-1)


def solution(mesh):
    one, rows, plate = P(AXES), P(AXES, None), P(None, AXES, None)
    return jax.shard_map(
        on_device,
        mesh=mesh,
        in_specs=(P(None, AXES), one, rows, one, one, rows, one, one, plate, plate),
        out_specs=(one, plate, one),
        check_vma=False,
    )
```

```python
import functools
import jax
import jax.numpy as jnp
from jax import lax
from jax.experimental import pallas as pl
from jax.experimental.pallas import tpu as pltpu
from jax.sharding import PartitionSpec as P

F32, BF16, I32 = jnp.float32, jnp.bfloat16, jnp.int32
TILE = 128
SUBSTEPS = 6
SLOTS = 32
HEAT_RATE = 0.004
WALL_HEAT = 0.5
UNROLL = 8
CHUNKS = 4
AXES = ("fluid", "sub")
VMEM_SPEC = pl.BlockSpec(memory_space=pltpu.VMEM)
SMEM_SPEC = pl.BlockSpec(memory_space=pltpu.SMEM)
ANY_SPEC = pl.BlockSpec(memory_space=pl.ANY)


def split3(x):
    high = x.astype(BF16).astype(F32)
    rest = x - high
    mid = rest.astype(BF16).astype(F32)
    return high, mid, rest - mid


def row_of(ref):
    return jnp.concatenate([ref[t : t + 1, :] for t in range(ref.shape[0])], axis=1)


def onehot(rows, codes, dtype=BF16):
    shape = (rows, codes.shape[1])
    hit = lax.broadcasted_iota(I32, shape, 0) == jnp.broadcast_to(codes, shape)
    return jnp.where(hit, 1.0, 0.0).astype(dtype)


def dot_nn(a, b):
    return lax.dot_general(a, b, (((1,), (0,)), ((), ())), preferred_element_type=F32)


def dot_nt(a, b):
    return lax.dot_general(a, b, (((1,), (1,)), ((), ())), preferred_element_type=F32)


def put_features(pos, temp_row, left, right):
    wide = pos.shape[1]
    moved = pos - 0.5
    high, mid, low = split3(moved)
    squares = jnp.sum(moved * moved, axis=0, keepdims=True)
    one = jnp.ones((3, wide), F32)
    minus = split3(-squares)
    temps = split3(temp_row)
    for place, part in enumerate((high, high, mid, mid, high, low)):
        left[3 * place : 3 * place + 3, :] = part
    left[18:21, :] = one
    for k in range(3):
        left[21 + k : 22 + k, :] = minus[k]
        left[24 + k : 25 + k, :] = temps[k]
    left[27:30, :] = one
    left[30:32, :] = jnp.zeros((2, wide), F32)
    if right is None:
        return
    base = split3(1.0 - squares)
    for place, part in enumerate((high, mid, high, mid, low, high)):
        right[3 * place : 3 * place + 3, :] = 2.0 * part
    right[21:24, :] = one
    right[24:27, :] = one
    for k in range(3):
        right[18 + k : 19 + k, :] = base[k]
        right[27 + k : 28 + k, :] = -temps[k]
    right[30:32, :] = jnp.zeros((2, wide), F32)


def ranks(owners, devices):
    row = lax.broadcasted_iota(I32, (TILE, 2 * TILE), 0)
    col = lax.broadcasted_iota(I32, (TILE, 2 * TILE), 1)
    before = jnp.where((row < col) | (col >= TILE), 1.0, 0.0).astype(BF16)
    so_far = jnp.zeros((devices, TILE), F32)
    out = []
    for t in range(owners.shape[1] // TILE):
        mine = owners[:, t * TILE : (t + 1) * TILE]
        counted = dot_nn(mine, before)
        out.append(jnp.sum(mine.astype(F32) * (counted[:, :TILE] + so_far), axis=0, keepdims=True))
        so_far = so_far + counted[:, TILE:]
    return jnp.concatenate(out, axis=1)


def plate_row(code):
    return (lax.shift_right_logical(code, 7) & 15) * 16 + lax.shift_right_logical(code, 11)


LOW, TOP = 7, 8


def stencil_weights():
    row = lax.broadcasted_iota(I32, (2 * TILE, 2 * TILE), 0) & (TILE - 1)
    col = lax.broadcasted_iota(I32, (2 * TILE, 2 * TILE), 1)
    lane = col & (TILE - 1)
    near = jnp.where(jnp.abs(row - lane) == 1, 1.0, jnp.where(row == lane, -6.0, 0.0))
    swap = jnp.where((jnp.abs(row - lane) == TILE - 1), 1.0, 0.0)
    return jnp.where(col < TILE, near, swap).astype(BF16)


MESH = pl.DeviceIdType.MESH


def step_kernel(
    fluids, subs, codes, own_pos, own_temp, code_rows, count, which, owner, cell, seen, temp, coef,
    heated, out, ghost_out,
    left, right, lefts, rights, partial, near_pos, near_temp, owners, rank_row, send, recv, hot, lows, source,
    values, back, cur, nxt, coefs, weights,
    near_send, near_recv, first_send, first_recv, last_send, last_recv, own_sem, load_sem, out_sem, send_sem, recv_sem,
):
    devices = fluids * subs
    layers, rows, span = temp.shape
    blocks = span // TILE
    tiles = own_temp.shape[0]
    deep = layers // CHUNKS
    fluid, sub = lax.axis_index(AXES[0]), lax.axis_index(AXES[1])
    me = fluid * subs + sub

    def place(index):
        return (lax.div(index, subs), lax.rem(index, subs))

    def everyone(act):
        for by in range(1, subs):
            act(fluid, lax.rem(sub + by, subs))

        def row(up, _):
            other = lax.rem(fluid + up, fluids)
            for by in range(subs):
                act(other, lax.rem(sub + by, subs))
            return 0

        lax.fori_loop(1, fluids, row, 0)

    loads = []
    for array, buf, offset in ((temp, cur, 1), (coef, coefs, 0)):
        for zt in range(blocks):
            at = pl.ds(zt * TILE, TILE)
            where = pl.ds(TOP, rows) if offset else pl.ds(0, rows)
            loads.append(pltpu.make_async_copy(
                array.at[:, :, at], buf.at[pl.ds(offset, layers), zt, where, :], load_sem.at[1 - offset, zt]))
    for load in loads:
        load.start()

    barrier = pltpu.get_barrier_semaphore()
    everyone(lambda f, s: pl.semaphore_signal(barrier, inc=1, device_id=(f, s), device_id_type=MESH))

    weights[...] = stencil_weights()
    for l in (0, layers + 1):
        for buf in (cur, nxt):
            for zt in range(blocks):
                buf[l, zt, TOP : TOP + rows, :] = jnp.zeros((rows, TILE), F32)

    for edge, x in ((0, LOW), (devices - 1, TOP + rows)):
        @pl.when(me == edge)
        def _():
            def wipe(l, _):
                for buf in (cur, nxt):
                    for zt in range(blocks):
                        buf[l, zt, x : x + 1, :] = jnp.zeros((1, TILE), F32)
                return 0

            lax.fori_loop(1, layers + 1, wipe, 0)

    put_features(own_pos[...], row_of(own_temp), left, right)
    for t in range(tiles):
        lefts[t] = left[:, t * TILE : (t + 1) * TILE].T.astype(BF16)
        block = right[:, t * TILE : (t + 1) * TILE]
        upper = lax.broadcasted_iota(I32, block.shape, 0) < 24
        rights[t, :, 0:TILE] = jnp.where(upper, block, 0.0).astype(BF16)
        rights[t, :, TILE : 2 * TILE] = jnp.where(upper, 0.0, block).astype(BF16)

    def halo(k, side, c):
        buf = (cur, nxt)[k % 2]
        x, y = ((TOP, TOP + rows), (TOP + rows - 1, LOW))[side]
        at = pl.ds(1 + c * deep, deep)
        return pltpu.make_async_remote_copy(
            src_ref=buf.at[at, :, pl.ds(x, 1), :], dst_ref=buf.at[at, :, pl.ds(y, 1), :],
            send_sem=send_sem.at[k, side, c], recv_sem=recv_sem.at[k, 1 - side, c],
            device_id=place(me - 1 if side == 0 else me + 1), device_id_type=MESH)

    has = (me > 0, me < devices - 1)

    def each(act):
        for side in (0, 1):
            @pl.when(has[side])
            def _():
                act(side)

    def launch(k, c):
        each(lambda side: halo(k, side, c).start())

    def arrive(k, c):
        each(lambda side: halo(k, 1 - side, c).wait_recv())

    def drain(k, c):
        each(lambda side: halo(k, side, c).wait_send())

    pl.semaphore_wait(barrier, devices - 1)
    behind = (fluid, lax.rem(sub + subs - 1, subs))
    near = [pltpu.make_async_remote_copy(
        src_ref=src, dst_ref=dst, send_sem=near_send.at[n], recv_sem=near_recv.at[n], device_id=behind,
        device_id_type=MESH) for n, (src, dst) in enumerate(((own_pos, near_pos), (own_temp, near_temp)))]
    for copy in near:
        copy.start()
    for load in loads[:blocks]:
        load.wait()
    for c in range(CHUNKS):
        launch(0, c)

    owners[...] = onehot(devices, row_of(owner))
    rank_row[...] = ranks(owners[...], devices)

    for copy in near:
        copy.wait_recv()
    put_features(near_pos[...], row_of(near_temp), left, None)
    for t in range(tiles):
        lefts[tiles + t] = left[:, t * TILE : (t + 1) * TILE].T.astype(BF16)

    def pair_group(group, _):
        for k in range(UNROLL):
            number = group * UNROLL + k
            code = codes[number]
            first = lax.shift_right_logical(code, 5) & (tiles - 1)
            second = code & (2 * tiles - 1)
            both = dot_nn(lefts[second], rights[first])
            close = jnp.maximum(both[:, :TILE], 0.0)
            gained = close * close * both[:, TILE:]
            partial[pl.ds(pl.multiple_of(number * 8, 8), 8), :] = jnp.sum(gained.reshape(TILE // 8, 8, TILE), axis=0)
        return 0

    pairs = codes.shape[0]
    lax.fori_loop(0, pairs // UNROLL, pair_group, 0)
    summed = partial[pl.ds(0, pairs, stride=8), :]
    for s in range(1, 8):
        summed = summed + partial[pl.ds(s, pairs, stride=8), :]
    code_row = row_of(code_rows)
    number = lax.broadcasted_iota(I32, code_row.shape, 1)
    first = jnp.where(number < count[0], lax.shift_right_logical(code_row, 5) & (tiles - 1), -1)
    firsts = onehot(tiles, first)
    gain = jnp.zeros((tiles, TILE), F32)
    for part in split3(summed):
        gain = gain + dot_nn(firsts, part.astype(BF16))
    out_temp = own_temp[...] + HEAT_RATE * gain
    heated[...] = out_temp

    parts = jnp.concatenate(split3(out_temp), axis=0).T.astype(BF16)
    which_row = row_of(which)
    high = onehot(tiles, lax.shift_right_logical(which_row, 7))
    picked = dot_nn(parts, jnp.concatenate([high] * 3, axis=0))
    low = jnp.broadcast_to(which_row & (TILE - 1), picked.shape)
    hit = lax.broadcasted_iota(I32, picked.shape, 0) == low
    flux = WALL_HEAT * (jnp.sum(jnp.where(hit, picked, 0.0), axis=0, keepdims=True) - row_of(seen))
    slot = onehot(SLOTS, rank_row[...].astype(I32), F32)
    cell_row = row_of(cell)
    cells = ((cell_row & ~255).astype(F32), (cell_row & 255).astype(F32), None)
    total = jnp.zeros((devices, 2 * SLOTS), F32)
    for f, c in zip(split3(flux), cells):
        lower_half = jnp.zeros_like(slot) if c is None else slot * c
        total = total + dot_nt(owners[...], jnp.concatenate([slot * f, lower_half], axis=0).astype(BF16))
    send[...] = jnp.concatenate([total, jnp.zeros((devices, TILE - 2 * SLOTS), F32)], axis=1)

    def spread_out(src, dst, sends, recvs):
        everyone(lambda f, s: pltpu.make_async_remote_copy(
            src_ref=src.at[pl.ds(f * subs + s, 1)], dst_ref=dst.at[pl.ds(me, 1)], send_sem=sends, recv_sem=recvs,
            device_id=(f, s), device_id_type=MESH).start())
        return pltpu.make_async_remote_copy(
            src_ref=src.at[pl.ds(0, devices - 1)], dst_ref=dst.at[pl.ds(0, devices - 1)], send_sem=sends,
            recv_sem=recvs, device_id=behind, device_id_type=MESH)

    own = pltpu.make_async_copy(send.at[pl.ds(me, 1)], recv.at[pl.ds(me, 1)], own_sem.at[0])
    own.start()
    first_trip = spread_out(send, recv, first_send, first_recv)

    for load in loads[blocks:]:
        load.wait()
    lane = lax.broadcasted_iota(I32, (rows, TILE), 1)
    lower = lane < TILE // 2

    def advance(src, dst, c):
        def layer(n, _):
            l = c * deep + n
            high, low = [], []
            for zt in range(blocks):
                center = src[l + 1, zt, TOP : TOP + rows, :]
                part = center.astype(BF16)
                high.append(part)
                low.append((center - part.astype(F32)).astype(BF16))
            both = jnp.concatenate([jnp.concatenate(high, axis=0), jnp.concatenate(low, axis=0)], axis=1)
            both = dot_nn(both, weights[...])
            along = [both[zt * rows : (zt + 1) * rows, :TILE] for zt in range(blocks)]
            ends = [both[zt * rows : (zt + 1) * rows, TILE:] for zt in range(blocks)]
            nothing = jnp.zeros((rows, TILE), F32)
            for zt in range(blocks):
                end = jnp.where(lower, ends[zt - 1] if zt > 0 else nothing, ends[zt + 1] if zt + 1 < blocks else nothing)
                beside = src[l, zt, TOP : TOP + rows, :] + src[l + 2, zt, TOP : TOP + rows, :]
                beside = beside + (src[l + 1, zt, LOW : LOW + rows, :] + src[l + 1, zt, TOP + 1 : TOP + 1 + rows, :])
                beside = beside + (along[zt] + end)
                dst[l + 1, zt, TOP : TOP + rows, :] = src[l + 1, zt, TOP : TOP + rows, :] + coefs[l, zt] * beside
            return 0

        lax.fori_loop(0, deep, layer, 0, unroll=4)

    def heat_top(dst):
        for zt in range(blocks):
            dst[1, zt, TOP : TOP + rows, :] += source[zt * rows : (zt + 1) * rows, :]

    def step(k):
        src, dst = (cur, nxt) if k % 2 == 0 else (nxt, cur)

        def chunk(c, _):
            arrive(k, c)
            if k > 0:
                drain(k - 1, c)
            advance(src, dst, c)
            if k == 0:
                @pl.when(c > 0)
                def _():
                    launch(1, c)
            elif k + 1 < SUBSTEPS:
                @pl.when(c == 0)
                def _():
                    heat_top(dst)

                launch(k + 1, c)
            else:
                @pl.when(c == 0)
                def _():
                    heat_top(dst)
            return 0

        lax.fori_loop(0, CHUNKS, chunk, 0)

    def stores(c):
        at = pl.ds(c * deep, deep)
        return [pltpu.make_async_copy(
            cur.at[pl.ds(1 + c * deep, deep), zt, pl.ds(TOP, rows), :], out.at[at, :, pl.ds(zt * TILE, TILE)],
            out_sem.at[c, zt]) for zt in range(blocks)]

    step(0)

    own.wait()
    first_trip.wait_recv()
    turned = recv[...].T
    for s in range(SLOTS):
        code = turned[SLOTS + s : SLOTS + s + 1, :].astype(I32)
        flux = turned[s : s + 1, :] * (1.0 / SUBSTEPS)
        at = pl.ds(s * devices, devices)
        hot[:, at] = onehot(hot.shape[0], plate_row(code))
        low = onehot(TILE, code & (TILE - 1), F32)
        for k, part in enumerate(split3(flux)):
            lows[k, :, at] = (low * part).astype(BF16)
    total = dot_nt(hot[...], lows[0])
    total = total + dot_nt(hot[...], lows[1])
    source[...] = total + dot_nt(hot[...], lows[2])
    heat_top(nxt)
    launch(1, 0)

    for k in range(1, SUBSTEPS - 1):
        step(k)

    last = SUBSTEPS - 1
    arrive(last, 0)
    drain(last - 1, 0)
    advance(nxt, cur, 0)
    heat_top(cur)
    for store in stores(0):
        store.start()
    flat = jnp.concatenate([cur[1, zt, TOP : TOP + rows, :] for zt in range(blocks)], axis=0)
    wide = jnp.concatenate([flat[k : k + TILE, :].T for k in range(0, flat.shape[0], TILE)], axis=1)
    parts = [part.astype(BF16) for part in split3(wide)]
    found_rows = []
    for s in range(SLOTS):
        at = pl.ds(s * devices, devices)
        found = sum(dot_nn(part, hot[:, at]) for part in parts)
        code = turned[SLOTS + s : SLOTS + s + 1, :].astype(I32)
        low = lax.broadcasted_iota(I32, found.shape, 0) == jnp.broadcast_to(code & (TILE - 1), found.shape)
        found_rows.append(jnp.sum(jnp.where(low, found, 0.0), axis=0, keepdims=True))
    found_rows.append(jnp.zeros((TILE - SLOTS, devices), F32))
    values[...] = jnp.concatenate(found_rows, axis=0).T
    own = pltpu.make_async_copy(values.at[pl.ds(me, 1)], back.at[pl.ds(me, 1)], own_sem.at[1])
    own.start()
    last_trip = spread_out(values, back, last_send, last_recv)

    def closing(c, _):
        arrive(last, c)
        drain(last - 1, c)
        advance(nxt, cur, c)
        for store in stores(c):
            store.start()
        return 0

    lax.fori_loop(1, CHUNKS, closing, 0)

    own.wait()
    last_trip.wait_recv()
    found = dot_nn(jnp.concatenate(split3(back[...].T[0:SLOTS, :]), axis=0).astype(BF16), owners[...])
    found = found[0:SLOTS] + found[SLOTS : 2 * SLOTS] + found[2 * SLOTS :]
    slot = onehot(SLOTS, rank_row[...].astype(I32), F32)
    ghost = jnp.sum(found * slot, axis=0, keepdims=True)
    for t in range(ghost_out.shape[0]):
        ghost_out[t : t + 1, :] = ghost[:, t * TILE : (t + 1) * TILE]

    for copy in near:
        copy.wait_send()
    first_trip.wait_send()
    last_trip.wait_send()
    for c in range(CHUNKS):
        drain(last, c)
    for c in range(CHUNKS):
        for store in stores(c):
            store.wait()


def call_step(codes, count, own_pos, own_temp, which, owner, cell, seen, temp, coef, fluids, subs):
    devices = fluids * subs
    layers, rows, span = temp.shape
    blocks = span // TILE
    tiles, wide = own_temp.shape[0], own_pos.shape[1]
    ghosts = owner.shape[0] * TILE
    DMA = pltpu.SemaphoreType.DMA
    return pl.pallas_call(
        functools.partial(step_kernel, fluids, subs),
        out_shape=(
            jax.ShapeDtypeStruct(own_temp.shape, F32),
            jax.ShapeDtypeStruct(temp.shape, F32),
            jax.ShapeDtypeStruct(owner.shape, F32),
        ),
        in_specs=[SMEM_SPEC] + [VMEM_SPEC] * 3 + [SMEM_SPEC] + [VMEM_SPEC] * 4 + [ANY_SPEC] * 2,
        out_specs=(VMEM_SPEC, ANY_SPEC, VMEM_SPEC),
        scratch_shapes=[
            pltpu.VMEM((32, wide), F32),
            pltpu.VMEM((32, wide), F32),
            pltpu.VMEM((2 * tiles, TILE, 32), BF16),
            pltpu.VMEM((tiles, 32, 2 * TILE), BF16),
            pltpu.VMEM((codes.shape[0] * 8, TILE), F32),
            pltpu.VMEM(own_pos.shape, F32),
            pltpu.VMEM(own_temp.shape, F32),
            pltpu.VMEM((devices, ghosts), BF16),
            pltpu.VMEM((1, ghosts), F32),
            pltpu.VMEM((devices, TILE), F32),
            pltpu.VMEM((devices, TILE), F32),
            pltpu.VMEM((rows * blocks, devices * SLOTS), BF16),
            pltpu.VMEM((3, TILE, devices * SLOTS), BF16),
            pltpu.VMEM((rows * blocks, TILE), F32),
            pltpu.VMEM((devices, TILE), F32),
            pltpu.VMEM((devices, TILE), F32),
            pltpu.VMEM((layers + 2, blocks, TOP + rows + 8, TILE), F32),
            pltpu.VMEM((layers + 2, blocks, TOP + rows + 8, TILE), F32),
            pltpu.VMEM((layers, blocks, rows, TILE), F32),
            pltpu.VMEM((2 * TILE, 2 * TILE), BF16),
            DMA((2,)),
            DMA((2,)),
            DMA,
            DMA,
            DMA,
            DMA,
            DMA((2,)),
            DMA((2, blocks)),
            DMA((CHUNKS, blocks)),
            DMA((SUBSTEPS, 2, CHUNKS)),
            DMA((SUBSTEPS, 2, CHUNKS)),
        ],
        compiler_params=pltpu.CompilerParams(collective_id=0, has_side_effects=True, vmem_limit_bytes=60 << 20),
        name="step",
    )(codes, own_pos, own_temp, codes.reshape(-1, TILE), count, which, owner, cell, seen, temp, coef)


def on_device(positions, particle_temp, pair_list, pair_count, ghost_particle, ghost_owner, ghost_cell,
              wall_seen, solid_temp, conduct):
    codes = pair_list[:, 0] * 32 + pair_list[:, 1]

    def tiled(x):
        return x.reshape(-1, TILE)

    heated, temp, ghost = call_step(
        codes, pair_count, positions, tiled(particle_temp), tiled(ghost_particle), tiled(ghost_owner),
        tiled(ghost_cell), tiled(wall_seen), solid_temp, conduct, lax.axis_size(AXES[0]), lax.axis_size(AXES[1]))
    return heated.reshape(-1), temp, ghost.reshape(-1)


def solution(mesh):
    one, rows, plate = P(AXES), P(AXES, None), P(None, AXES, None)
    return jax.shard_map(
        on_device,
        mesh=mesh,
        in_specs=(P(None, AXES), one, rows, one, one, rows, one, one, plate, plate),
        out_specs=(one, plate, one),
        check_vma=False,
    )
```

```python
import functools
import jax
import jax.numpy as jnp
from jax import lax
from jax.experimental import pallas as pl
from jax.experimental.pallas import tpu as pltpu
from jax.sharding import PartitionSpec as P

F32, BF16, I32 = jnp.float32, jnp.bfloat16, jnp.int32
TILE = 128
SUBSTEPS = 6
SLOTS = 32
HEAT_RATE = 0.004
WALL_HEAT = 0.5
UNROLL = 16
CHUNKS = 4
AXES = ("fluid", "sub")
VMEM_SPEC = pl.BlockSpec(memory_space=pltpu.VMEM)
SMEM_SPEC = pl.BlockSpec(memory_space=pltpu.SMEM)
ANY_SPEC = pl.BlockSpec(memory_space=pl.ANY)
HBM_SPEC = pl.BlockSpec(memory_space=pltpu.HBM)


def split3(x):
    high = x.astype(BF16).astype(F32)
    rest = x - high
    mid = rest.astype(BF16).astype(F32)
    return high, mid, rest - mid


def split2(x):
    high = x.astype(BF16).astype(F32)
    return high, x - high


def row_of(ref):
    return jnp.concatenate([ref[t : t + 1, :] for t in range(ref.shape[0])], axis=1)


def onehot(rows, codes, dtype=BF16):
    shape = (rows, codes.shape[1])
    hit = lax.broadcasted_iota(I32, shape, 0) == jnp.broadcast_to(codes, shape)
    return jnp.where(hit, 1.0, 0.0).astype(dtype)


def dot_nn(a, b):
    return lax.dot_general(a, b, (((1,), (0,)), ((), ())), preferred_element_type=F32)


def dot_nt(a, b):
    return lax.dot_general(a, b, (((1,), (1,)), ((), ())), preferred_element_type=F32)


def put_features(pos, temp_row, left, right):
    wide = pos.shape[1]
    moved = pos - 0.5
    high, mid, low = split3(moved)
    squares = jnp.sum(moved * moved, axis=0, keepdims=True)
    one = jnp.ones((3, wide), F32)
    minus = split3(-squares)
    temps = split3(temp_row)
    for place, part in enumerate((high, high, mid, mid, high, low)):
        left[3 * place : 3 * place + 3, :] = part
    left[18:21, :] = one
    for k in range(3):
        left[21 + k : 22 + k, :] = minus[k]
        left[24 + k : 25 + k, :] = temps[k]
    left[27:32, :] = jnp.zeros((5, wide), F32)
    if right is None:
        return
    base = split3(1.0 - squares)
    for place, part in enumerate((high, mid, high, mid, low, high)):
        right[3 * place : 3 * place + 3, :] = 2.0 * part
    for k in range(3):
        right[18 + k : 19 + k, :] = base[k]
    right[21:24, :] = one
    right[24:32, :] = jnp.zeros((8, wide), F32)


def put_tile(left, t, tile, lefts, across):
    block = left[:, t * TILE : (t + 1) * TILE]
    block = jnp.concatenate([block] * 4, axis=0).T
    lane = lax.broadcasted_iota(I32, block.shape, 1)
    lefts[0, tile] = jnp.where(lane < 32, block, 0.0).astype(BF16)
    lefts[1, tile] = jnp.where((lane >= 32) & (lane < 64), block, 0.0).astype(BF16)
    row = lax.broadcasted_iota(I32, (TILE, TILE), 0)
    take = jnp.where((row >= 24) & (row < 27), 1.0, 0.0).astype(BF16)
    across[tile] = dot_nn(lefts[0, tile], take)


def ranks(owners, devices):
    row = lax.broadcasted_iota(I32, (TILE, 2 * TILE), 0)
    col = lax.broadcasted_iota(I32, (TILE, 2 * TILE), 1)
    before = jnp.where((row < col) | (col >= TILE), 1.0, 0.0).astype(BF16)
    so_far = jnp.zeros((devices, TILE), F32)
    out = []
    for t in range(owners.shape[1] // TILE):
        mine = owners[:, t * TILE : (t + 1) * TILE]
        counted = dot_nn(mine, before)
        out.append(jnp.sum(mine.astype(F32) * (counted[:, :TILE] + so_far), axis=0, keepdims=True))
        so_far = so_far + counted[:, TILE:]
    return jnp.concatenate(out, axis=1)


def plate_row(code):
    return (lax.shift_right_logical(code, 7) & 15) * 16 + lax.shift_right_logical(code, 11)


LOW, TOP = 7, 8


def stencil_weights():
    row = lax.broadcasted_iota(I32, (2 * TILE, 2 * TILE), 0) & (TILE - 1)
    col = lax.broadcasted_iota(I32, (2 * TILE, 2 * TILE), 1)
    lane = col & (TILE - 1)
    near = jnp.where(jnp.abs(row - lane) == 1, 1.0, jnp.where(row == lane, -6.0, 0.0))
    swap = jnp.where((jnp.abs(row - lane) == TILE - 1), 1.0, 0.0)
    return jnp.where(col < TILE, near, swap).astype(BF16)


MESH = pl.DeviceIdType.MESH


def step_kernel(
    fluids, subs, count, codes_in, pos_in, temp_in, which_in, owner_in, cell_in, seen_in, temp, coef,
    heated, out, ghost_out,
    codes, code_rows, own_pos, own_temp, which, owner, cell, seen, small_sem,
    left, right, lefts, across, rights, partial, near_pos, near_temp, owners, rank_row, send, recv, turned, found_rows, hot, lows, source,
    values, back, cur, nxt, coefs, weights,
    near_send, near_recv, first_send, first_recv, last_send, last_recv, own_sem, load_sem, send_sem, recv_sem,
):
    devices = fluids * subs
    layers, rows, span = temp.shape
    blocks = span // TILE
    tiles = own_temp.shape[0]
    deep = layers // CHUNKS
    fluid, sub = lax.axis_index(AXES[0]), lax.axis_index(AXES[1])
    me = fluid * subs + sub

    def place(index):
        return (lax.div(index, subs), lax.rem(index, subs))

    def everyone(act):
        for by in range(1, subs):
            act(fluid, lax.rem(sub + by, subs))

        def row(up, _):
            other = lax.rem(fluid + up, fluids)
            for by in range(subs):
                act(other, lax.rem(sub + by, subs))
            return 0

        lax.fori_loop(1, fluids, row, 0)

    small = [pltpu.make_async_copy(src, dst, small_sem.at[n]) for n, (src, dst) in enumerate((
        (codes_in, codes), (codes_in, code_rows), (pos_in, own_pos), (temp_in, own_temp), (which_in, which),
        (owner_in, owner), (cell_in, cell), (seen_in, seen)))]
    for copy in small:
        copy.start()

    loads = []
    for array, buf, offset in ((temp, cur, 1), (coef, coefs, 0)):
        for zt in range(blocks):
            at = pl.ds(zt * TILE, TILE)
            where = pl.ds(TOP, rows) if offset else pl.ds(0, rows)
            loads.append(pltpu.make_async_copy(
                array.at[:, :, at], buf.at[pl.ds(offset, layers), zt, where, :], load_sem.at[1 - offset, zt]))
    for load in loads:
        load.start()

    barrier = pltpu.get_barrier_semaphore()
    everyone(lambda f, s: pl.semaphore_signal(barrier, inc=1, device_id=(f, s), device_id_type=MESH))

    weights[...] = stencil_weights()
    for l in (0, layers + 1):
        for buf in (cur, nxt):
            for zt in range(blocks):
                buf[l, zt, TOP : TOP + rows, :] = jnp.zeros((rows, TILE), F32)

    for edge, x in ((0, LOW), (devices - 1, TOP + rows)):
        @pl.when(me == edge)
        def _():
            def wipe(l, _):
                for buf in (cur, nxt):
                    for zt in range(blocks):
                        buf[l, zt, x : x + 1, :] = jnp.zeros((1, TILE), F32)
                return 0

            lax.fori_loop(1, layers + 1, wipe, 0)

    for copy in small:
        copy.wait()
    put_features(own_pos[...], row_of(own_temp), left, right)
    for t in range(tiles):
        put_tile(left, t, t, lefts, across)
        rights[t] = right[:, t * TILE : (t + 1) * TILE].astype(BF16)

    def halo(k, side, c):
        buf = (cur, nxt)[k % 2]
        x, y = ((TOP, TOP + rows), (TOP + rows - 1, LOW))[side]
        at = pl.ds(1 + c * deep, deep)
        return pltpu.make_async_remote_copy(
            src_ref=buf.at[at, :, pl.ds(x, 1), :], dst_ref=buf.at[at, :, pl.ds(y, 1), :],
            send_sem=send_sem.at[k, side, c], recv_sem=recv_sem.at[k, 1 - side, c],
            device_id=place(me - 1 if side == 0 else me + 1), device_id_type=MESH)

    has = (me > 0, me < devices - 1)

    def each(act):
        for side in (0, 1):
            @pl.when(has[side])
            def _():
                act(side)

    def launch(k, c):
        each(lambda side: halo(k, side, c).start())

    def arrive(k, c):
        each(lambda side: halo(k, 1 - side, c).wait_recv())

    def drain(k, c):
        each(lambda side: halo(k, side, c).wait_send())

    pl.semaphore_wait(barrier, devices - 1)
    behind = (fluid, lax.rem(sub + subs - 1, subs))
    near = [pltpu.make_async_remote_copy(
        src_ref=src, dst_ref=dst, send_sem=near_send.at[n], recv_sem=near_recv.at[n], device_id=behind,
        device_id_type=MESH) for n, (src, dst) in enumerate(((own_pos, near_pos), (own_temp, near_temp)))]
    for copy in near:
        copy.start()
    for load in loads[:blocks]:
        load.wait()
    for c in range(CHUNKS):
        launch(0, c)

    owners[...] = onehot(devices, row_of(owner))
    rank_row[...] = ranks(owners[...], devices)

    for copy in near:
        copy.wait_recv()
    put_features(near_pos[...], row_of(near_temp), left, None)
    for t in range(tiles):
        put_tile(left, t, tiles + t, lefts, across)

    none = jnp.zeros((32, TILE), BF16)

    def pair_group(group, _):
        for k in range(0, UNROLL, 2):
            number = group * UNROLL + k
            first = [codes[0, number + n] & (tiles - 1) for n in (0, 1)]
            second = [codes[1, number + n] & (2 * tiles - 1) for n in (0, 1)]
            stacked = jnp.concatenate([
                jnp.concatenate([rights[first[0]], none], axis=1),
                jnp.concatenate([none, rights[first[1]]], axis=1)], axis=0)
            both = dot_nn(lefts[0, second[0], :, 0:64] + lefts[1, second[1], :, 0:64], stacked)
            for n in (0, 1):
                close = jnp.maximum(both[:, n * TILE : (n + 1) * TILE], 0.0)
                gained = (close * close) * (across[second[n]] - own_temp[pl.ds(first[n], 1), :])
                at = pl.multiple_of((number + n) * 8, 8)
                partial[pl.ds(at, 8), :] = jnp.sum(gained.reshape(TILE // 8, 8, TILE), axis=0)
        return 0

    pairs = codes.shape[1]
    lax.fori_loop(0, pairs // UNROLL, pair_group, 0)
    summed = partial[pl.ds(0, pairs, stride=8), :]
    for s in range(1, 8):
        summed = summed + partial[pl.ds(s, pairs, stride=8), :]
    code_row = code_rows[0:1, :]
    number = lax.broadcasted_iota(I32, code_row.shape, 1)
    first = jnp.where(number < count[0], code_row & (tiles - 1), -1)
    firsts = onehot(tiles, first)
    gain = jnp.zeros((tiles, TILE), F32)
    for part in split3(summed):
        gain = gain + dot_nn(firsts, part.astype(BF16))
    out_temp = own_temp[...] + HEAT_RATE * gain
    heated[...] = out_temp

    parts = jnp.concatenate(split3(out_temp), axis=0).T.astype(BF16)
    which_row = row_of(which)
    high = onehot(tiles, lax.shift_right_logical(which_row, 7))
    picked = dot_nn(parts, jnp.concatenate([high] * 3, axis=0))
    low = jnp.broadcast_to(which_row & (TILE - 1), picked.shape)
    hit = lax.broadcasted_iota(I32, picked.shape, 0) == low
    flux = WALL_HEAT * (jnp.sum(jnp.where(hit, picked, 0.0), axis=0, keepdims=True) - row_of(seen))
    slot = onehot(SLOTS, rank_row[...].astype(I32), F32)
    cell_row = row_of(cell)
    cells = ((cell_row & ~255).astype(F32), (cell_row & 255).astype(F32), None)
    total = jnp.zeros((devices, 2 * SLOTS), F32)
    for f, c in zip(split3(flux), cells):
        lower_half = jnp.zeros_like(slot) if c is None else slot * c
        total = total + dot_nt(owners[...], jnp.concatenate([slot * f, lower_half], axis=0).astype(BF16))
    send[...] = jnp.concatenate([total, jnp.zeros((devices, TILE - 2 * SLOTS), F32)], axis=1)

    def spread_out(src, dst, sends, recvs):
        everyone(lambda f, s: pltpu.make_async_remote_copy(
            src_ref=src.at[pl.ds(f * subs + s, 1)], dst_ref=dst.at[pl.ds(me, 1)], send_sem=sends, recv_sem=recvs,
            device_id=(f, s), device_id_type=MESH).start())
        return pltpu.make_async_remote_copy(
            src_ref=src.at[pl.ds(0, devices - 1)], dst_ref=dst.at[pl.ds(0, devices - 1)], send_sem=sends,
            recv_sem=recvs, device_id=behind, device_id_type=MESH)

    own = pltpu.make_async_copy(send.at[pl.ds(me, 1)], recv.at[pl.ds(me, 1)], own_sem.at[0])
    own.start()
    first_trip = spread_out(send, recv, first_send, first_recv)

    for load in loads[blocks:]:
        load.wait()
    lane = lax.broadcasted_iota(I32, (rows, TILE), 1)
    lower = lane < TILE // 2

    def advance(src, dst, c):
        def layer(n, _):
            l = c * deep + n
            high, low = [], []
            for zt in range(blocks):
                center = src[l + 1, zt, TOP : TOP + rows, :]
                part = center.astype(BF16)
                high.append(part)
                low.append((center - part.astype(F32)).astype(BF16))
            both = jnp.concatenate([jnp.concatenate(high, axis=0), jnp.concatenate(low, axis=0)], axis=1)
            both = dot_nn(both, weights[...])
            along = [both[zt * rows : (zt + 1) * rows, :TILE] for zt in range(blocks)]
            ends = [both[zt * rows : (zt + 1) * rows, TILE:] for zt in range(blocks)]
            nothing = jnp.zeros((rows, TILE), F32)
            for zt in range(blocks):
                end = jnp.where(lower, ends[zt - 1] if zt > 0 else nothing, ends[zt + 1] if zt + 1 < blocks else nothing)
                beside = src[l, zt, TOP : TOP + rows, :] + src[l + 2, zt, TOP : TOP + rows, :]
                beside = beside + (src[l + 1, zt, LOW : LOW + rows, :] + src[l + 1, zt, TOP + 1 : TOP + 1 + rows, :])
                beside = beside + (along[zt] + end)
                value = src[l + 1, zt, TOP : TOP + rows, :] + coefs[l, zt] * beside
                if dst is None:
                    out[l, :, zt * TILE : (zt + 1) * TILE] = value
                else:
                    dst[l + 1, zt, TOP : TOP + rows, :] = value
            return 0

        lax.fori_loop(0, deep, layer, 0, unroll=4)

    def heat_top(dst):
        for zt in range(blocks):
            dst[1, zt, TOP : TOP + rows, :] += source[zt * rows : (zt + 1) * rows, :]

    def step(k):
        src, dst = (cur, nxt) if k % 2 == 0 else (nxt, cur)

        def chunk(c, _):
            arrive(k, c)
            if k > 0:
                drain(k - 1, c)
            advance(src, dst, c)
            if k == 0:
                @pl.when(c > 0)
                def _():
                    launch(1, c)
            elif k + 1 < SUBSTEPS:
                @pl.when(c == 0)
                def _():
                    heat_top(dst)

                launch(k + 1, c)
            else:
                @pl.when(c == 0)
                def _():
                    heat_top(dst)
            return 0

        lax.fori_loop(0, CHUNKS, chunk, 0)

    step(0)

    own.wait()
    first_trip.wait_recv()
    turned[...] = recv[...].T

    def place_slot(n, _):
        for k in range(4):
            s = n * 4 + k
            code = turned[pl.ds(SLOTS + s, 1), :].astype(I32)
            flux = turned[pl.ds(s, 1), :] * (1.0 / SUBSTEPS)
            at = pl.ds(pl.multiple_of(s * devices, TILE), devices)
            hot[:, at] = onehot(hot.shape[0], plate_row(code))
            low = onehot(TILE, code & (TILE - 1), F32)
            for m, part in enumerate(split2(flux)):
                lows[m * TILE : (m + 1) * TILE, at] = (low * part).astype(BF16)
        return 0

    lax.fori_loop(0, SLOTS // 4, place_slot, 0, unroll=2)
    total = dot_nt(hot[...], lows[...])
    source[...] = total[:, :TILE] + total[:, TILE:]
    heat_top(nxt)
    launch(1, 0)

    for k in range(1, SUBSTEPS - 1):
        step(k)

    last = SUBSTEPS - 1
    arrive(last, 0)
    drain(last - 1, 0)
    advance(nxt, None, 0)
    for zt in range(blocks):
        out[0, :, zt * TILE : (zt + 1) * TILE] += source[zt * rows : (zt + 1) * rows, :]
    flat = jnp.concatenate([out[0, :, zt * TILE : (zt + 1) * TILE] for zt in range(blocks)], axis=0)
    wide = jnp.concatenate([flat[k : k + TILE, :].T for k in range(0, flat.shape[0], TILE)], axis=1)
    parts = jnp.concatenate(split2(wide), axis=0).astype(BF16)

    def pick_slots(n, _):
        for k in range(2):
            at = pl.ds(pl.multiple_of((n * 2 + k) * 2 * devices, TILE), 2 * devices)
            found = dot_nn(parts, hot[:, at])
            found = found[:TILE] + found[TILE:]
            s = n * 4 + k * 2
            code = jnp.concatenate([turned[pl.ds(SLOTS + s + m, 1), :] for m in (0, 1)], axis=1).astype(I32)
            low = lax.broadcasted_iota(I32, found.shape, 0) == jnp.broadcast_to(code & (TILE - 1), found.shape)
            value = jnp.sum(jnp.where(low, found, 0.0), axis=0, keepdims=True)
            for m in (0, 1):
                found_rows[pl.ds(s + m, 1), :] = value[:, m * devices : (m + 1) * devices]
        return 0

    found_rows[...] = jnp.zeros(found_rows.shape, F32)
    lax.fori_loop(0, SLOTS // 4, pick_slots, 0, unroll=2)
    values[...] = found_rows[...].T
    own = pltpu.make_async_copy(values.at[pl.ds(me, 1)], back.at[pl.ds(me, 1)], own_sem.at[1])
    own.start()
    last_trip = spread_out(values, back, last_send, last_recv)

    def closing(c, _):
        arrive(last, c)
        drain(last - 1, c)
        advance(nxt, None, c)
        return 0

    lax.fori_loop(1, CHUNKS, closing, 0)

    own.wait()
    last_trip.wait_recv()
    found = dot_nn(jnp.concatenate(split3(back[...].T[0:SLOTS, :]), axis=0).astype(BF16), owners[...])
    found = found[0:SLOTS] + found[SLOTS : 2 * SLOTS] + found[2 * SLOTS :]
    slot = onehot(SLOTS, rank_row[...].astype(I32), F32)
    ghost = jnp.sum(found * slot, axis=0, keepdims=True)
    for t in range(ghost_out.shape[0]):
        ghost_out[t : t + 1, :] = ghost[:, t * TILE : (t + 1) * TILE]

    for copy in near:
        copy.wait_send()
    first_trip.wait_send()
    last_trip.wait_send()
    for c in range(CHUNKS):
        drain(last, c)


def call_step(codes, count, own_pos, own_temp, which, owner, cell, seen, temp, coef, fluids, subs):
    devices = fluids * subs
    layers, rows, span = temp.shape
    blocks = span // TILE
    tiles, wide = own_temp.shape[0], own_pos.shape[1]
    ghosts = owner.shape[0] * TILE
    DMA = pltpu.SemaphoreType.DMA
    return pl.pallas_call(
        functools.partial(step_kernel, fluids, subs),
        out_shape=(
            jax.ShapeDtypeStruct(own_temp.shape, F32),
            pltpu.VMEM(temp.shape, F32),
            jax.ShapeDtypeStruct(owner.shape, F32),
        ),
        in_specs=[SMEM_SPEC] + [HBM_SPEC] * 9,
        out_specs=(VMEM_SPEC,) * 3,
        scratch_shapes=[
            pltpu.SMEM(codes.shape, I32),
            pltpu.VMEM(codes.shape, I32),
            pltpu.VMEM(own_pos.shape, F32),
            pltpu.VMEM(own_temp.shape, F32),
            pltpu.VMEM(which.shape, I32),
            pltpu.VMEM(owner.shape, I32),
            pltpu.VMEM(cell.shape, I32),
            pltpu.VMEM(seen.shape, F32),
            DMA((8,)),
            pltpu.VMEM((32, wide), F32),
            pltpu.VMEM((32, wide), F32),
            pltpu.VMEM((2, 2 * tiles, TILE, TILE), BF16),
            pltpu.VMEM((2 * tiles, TILE, TILE), F32),
            pltpu.VMEM((tiles, 32, TILE), BF16),
            pltpu.VMEM((codes.shape[1] * 8, TILE), F32),
            pltpu.VMEM(own_pos.shape, F32),
            pltpu.VMEM(own_temp.shape, F32),
            pltpu.VMEM((devices, ghosts), BF16),
            pltpu.VMEM((1, ghosts), F32),
            pltpu.VMEM((devices, TILE), F32),
            pltpu.VMEM((devices, TILE), F32),
            pltpu.VMEM((TILE, devices), F32),
            pltpu.VMEM((TILE, devices), F32),
            pltpu.VMEM((rows * blocks, devices * SLOTS), BF16),
            pltpu.VMEM((2 * TILE, devices * SLOTS), BF16),
            pltpu.VMEM((rows * blocks, TILE), F32),
            pltpu.VMEM((devices, TILE), F32),
            pltpu.VMEM((devices, TILE), F32),
            pltpu.VMEM((layers + 2, blocks, TOP + rows + 8, TILE), F32),
            pltpu.VMEM((layers + 2, blocks, TOP + rows + 8, TILE), F32),
            pltpu.VMEM((layers, blocks, rows, TILE), F32),
            pltpu.VMEM((2 * TILE, 2 * TILE), BF16),
            DMA((2,)),
            DMA((2,)),
            DMA,
            DMA,
            DMA,
            DMA,
            DMA((2,)),
            DMA((2, blocks)),
            DMA((SUBSTEPS, 2, CHUNKS)),
            DMA((SUBSTEPS, 2, CHUNKS)),
        ],
        compiler_params=pltpu.CompilerParams(collective_id=0, has_side_effects=True, vmem_limit_bytes=48 << 20),
        name="step",
    )(count, *[pltpu.with_memory_space_constraint(x, pltpu.HBM) for x in (
        codes, own_pos, own_temp, which, owner, cell, seen, temp, coef)])


def on_device(positions, particle_temp, pair_list, pair_count, ghost_particle, ghost_owner, ghost_cell,
              wall_seen, solid_temp, conduct):
    codes = pair_list.T

    def tiled(x):
        return x.reshape(-1, TILE)

    heated, temp, ghost = call_step(
        codes, pair_count, positions, tiled(particle_temp), tiled(ghost_particle), tiled(ghost_owner),
        tiled(ghost_cell), tiled(wall_seen), solid_temp, conduct, lax.axis_size(AXES[0]), lax.axis_size(AXES[1]))
    return heated.reshape(-1), temp, ghost.reshape(-1)


def solution(mesh):
    one, rows, plate = P(AXES), P(AXES, None), P(None, AXES, None)
    return jax.shard_map(
        on_device,
        mesh=mesh,
        in_specs=(P(None, AXES), one, rows, one, one, rows, one, one, plate, plate),
        out_specs=(one, plate, one),
        check_vma=False,
    )
```

```python
import functools
import jax
import jax.numpy as jnp
from jax import lax
from jax.experimental import pallas as pl
from jax.experimental.pallas import tpu as pltpu
from jax.sharding import PartitionSpec as P

F32, BF16, I32 = jnp.float32, jnp.bfloat16, jnp.int32
TILE = 128
SUBSTEPS = 6
SLOTS = 32
HEAT_RATE = 0.004
WALL_HEAT = 0.5
UNROLL = 32
CHUNKS = 8
EARLY = 3
AXES = ("fluid", "sub")
VMEM_SPEC = pl.BlockSpec(memory_space=pltpu.VMEM)
SMEM_SPEC = pl.BlockSpec(memory_space=pltpu.SMEM)
ANY_SPEC = pl.BlockSpec(memory_space=pl.ANY)
HBM_SPEC = pl.BlockSpec(memory_space=pltpu.HBM)


def split3(x):
    high = x.astype(BF16).astype(F32)
    rest = x - high
    mid = rest.astype(BF16).astype(F32)
    return high, mid, rest - mid


def split2(x):
    high = x.astype(BF16).astype(F32)
    return high, x - high


def row_of(ref):
    return jnp.concatenate([ref[t : t + 1, :] for t in range(ref.shape[0])], axis=1)


def onehot(rows, codes, dtype=BF16):
    shape = (rows, codes.shape[1])
    hit = lax.broadcasted_iota(I32, shape, 0) == jnp.broadcast_to(codes, shape)
    return jnp.where(hit, 1.0, 0.0).astype(dtype)


def dot_nn(a, b):
    return lax.dot_general(a, b, (((1,), (0,)), ((), ())), preferred_element_type=F32)


def dot_nt(a, b):
    return lax.dot_general(a, b, (((1,), (1,)), ((), ())), preferred_element_type=F32)


def put_features(pos, temp_row, left, right):
    wide = pos.shape[1]
    moved = pos - 0.5
    high, mid, low = split3(moved)
    squares = jnp.sum(moved * moved, axis=0, keepdims=True)
    one = jnp.ones((3, wide), F32)
    minus = split3(-squares)
    temps = split3(temp_row)
    for place, part in enumerate((high, high, mid, mid, high, low)):
        left[3 * place : 3 * place + 3, :] = part
    left[18:21, :] = one
    for k in range(3):
        left[21 + k : 22 + k, :] = minus[k]
        left[24 + k : 25 + k, :] = temps[k]
    left[27:32, :] = jnp.zeros((5, wide), F32)
    if right is None:
        return
    base = split3(1.0 - squares)
    for place, part in enumerate((high, mid, high, mid, low, high)):
        right[3 * place : 3 * place + 3, :] = 2.0 * part
    for k in range(3):
        right[18 + k : 19 + k, :] = base[k]
    right[21:24, :] = one
    right[24:32, :] = jnp.zeros((8, wide), F32)


def put_tile(left, t, tile, lefts, across):
    block = left[:, t * TILE : (t + 1) * TILE]
    block = jnp.concatenate([block] * 4, axis=0).T
    lane = lax.broadcasted_iota(I32, block.shape, 1)
    lefts[0, tile] = jnp.where(lane < 32, block, 0.0).astype(BF16)
    lefts[1, tile] = jnp.where((lane >= 32) & (lane < 64), block, 0.0).astype(BF16)
    row = lax.broadcasted_iota(I32, (TILE, TILE), 0)
    take = jnp.where((row >= 24) & (row < 27), 1.0, 0.0).astype(BF16)
    across[tile] = dot_nn(lefts[0, tile], take)


def ranks(owners, devices):
    row = lax.broadcasted_iota(I32, (TILE, 2 * TILE), 0)
    col = lax.broadcasted_iota(I32, (TILE, 2 * TILE), 1)
    before = jnp.where((row < col) | (col >= TILE), 1.0, 0.0).astype(BF16)
    so_far = jnp.zeros((devices, TILE), F32)
    out = []
    for t in range(owners.shape[1] // TILE):
        mine = owners[:, t * TILE : (t + 1) * TILE]
        counted = dot_nn(mine, before)
        out.append(jnp.sum(mine.astype(F32) * (counted[:, :TILE] + so_far), axis=0, keepdims=True))
        so_far = so_far + counted[:, TILE:]
    return jnp.concatenate(out, axis=1)


def plate_row(code):
    return (lax.shift_right_logical(code, 7) & 15) * 16 + lax.shift_right_logical(code, 11)


LOW, TOP = 7, 8


def stencil_weights():
    row = lax.broadcasted_iota(I32, (2 * TILE, 2 * TILE), 0) & (TILE - 1)
    col = lax.broadcasted_iota(I32, (2 * TILE, 2 * TILE), 1)
    lane = col & (TILE - 1)
    near = jnp.where(jnp.abs(row - lane) == 1, 1.0, jnp.where(row == lane, -6.0, 0.0))
    swap = jnp.where((jnp.abs(row - lane) == TILE - 1), 1.0, 0.0)
    return jnp.where(col < TILE, near, swap).astype(BF16)


MESH = pl.DeviceIdType.MESH


def step_kernel(
    fluids, subs, count, codes_in, pos_in, temp_in, which_in, owner_in, cell_in, seen_in, temp, coef,
    heated, out, ghost_out,
    codes, code_rows, own_pos, own_temp, which, owner, cell, seen, small_sem,
    left, right, lefts, across, rights, partial, near_pos, near_temp, owners, rank_row, send, recv, turned, found_rows, hot, lows, source,
    values, back, cur, nxt, coefs, weights, wide_source, wide_coefs, resp, resp_next, side_send, side_recv,
    near_send, near_recv, first_send, first_recv, last_send, last_recv, own_sem, load_sem, send_sem, recv_sem,
):
    devices = fluids * subs
    layers, rows, span = temp.shape
    blocks = span // TILE
    tiles = own_temp.shape[0]
    deep = layers // CHUNKS
    fluid, sub = lax.axis_index(AXES[0]), lax.axis_index(AXES[1])
    me = fluid * subs + sub

    def place(index):
        return (lax.div(index, subs), lax.rem(index, subs))

    def everyone(act):
        for by in range(1, subs):
            act(fluid, lax.rem(sub + by, subs))

        def row(up, _):
            other = lax.rem(fluid + up, fluids)
            for by in range(subs):
                act(other, lax.rem(sub + by, subs))
            return 0

        lax.fori_loop(1, fluids, row, 0)

    small = [pltpu.make_async_copy(src, dst, small_sem.at[n]) for n, (src, dst) in enumerate((
        (codes_in, codes), (codes_in, code_rows), (pos_in, own_pos), (temp_in, own_temp), (which_in, which),
        (owner_in, owner), (cell_in, cell), (seen_in, seen)))]
    for copy in small:
        copy.start()

    loads = []
    for array, buf, offset in ((temp, cur, 1), (coef, coefs, 0)):
        for zt in range(blocks):
            at = pl.ds(zt * TILE, TILE)
            where = pl.ds(TOP, rows) if offset else pl.ds(0, rows)
            loads.append(pltpu.make_async_copy(
                array.at[:, :, at], buf.at[pl.ds(offset, layers), zt, where, :], load_sem.at[1 - offset, zt]))
    for load in loads:
        load.start()

    barrier = pltpu.get_barrier_semaphore()
    everyone(lambda f, s: pl.semaphore_signal(barrier, inc=1, device_id=(f, s), device_id_type=MESH))

    weights[...] = stencil_weights()
    for l in (0, layers + 1):
        for buf in (cur, nxt):
            for zt in range(blocks):
                buf[l, zt, TOP : TOP + rows, :] = jnp.zeros((rows, TILE), F32)

    for buf in (resp, resp_next):
        buf[...] = jnp.zeros(buf.shape, F32)

    for edge, x, far in ((0, LOW, 0), (devices - 1, TOP + rows, rows + 8)):
        @pl.when(me == edge)
        def _():
            wide_source[:, far : far + 8, :] = jnp.zeros((blocks, 8, TILE), F32)
            wide_coefs[:, :, far : far + 8, :] = jnp.zeros((EARLY, blocks, 8, TILE), F32)

            def wipe(l, _):
                for buf in (cur, nxt):
                    for zt in range(blocks):
                        buf[l, zt, x : x + 1, :] = jnp.zeros((1, TILE), F32)
                return 0

            lax.fori_loop(1, layers + 1, wipe, 0)

    for copy in small:
        copy.wait()
    put_features(own_pos[...], row_of(own_temp), left, right)
    for t in range(tiles):
        put_tile(left, t, t, lefts, across)
        rights[t] = right[:, t * TILE : (t + 1) * TILE].astype(BF16)

    def halo(k, side, c):
        buf = (cur, nxt)[k % 2]
        x, y = ((TOP, TOP + rows), (TOP + rows - 1, LOW))[side]
        at = pl.ds(1 + c * deep, deep)
        return pltpu.make_async_remote_copy(
            src_ref=buf.at[at, :, pl.ds(x, 1), :], dst_ref=buf.at[at, :, pl.ds(y, 1), :],
            send_sem=send_sem.at[k, side, c], recv_sem=recv_sem.at[k, 1 - side, c],
            device_id=place(me - 1 if side == 0 else me + 1), device_id_type=MESH)

    has = (me > 0, me < devices - 1)

    def each(act):
        for side in (0, 1):
            @pl.when(has[side])
            def _():
                act(side)

    def launch(k, c):
        each(lambda side: halo(k, side, c).start())

    def arrive(k, c):
        each(lambda side: halo(k, 1 - side, c).wait_recv())

    def drain(k, c):
        each(lambda side: halo(k, side, c).wait_send())

    def side_copy(n, side):
        at, to = ((pl.ds(0, 8), pl.ds(rows + 8, 8)), (pl.ds(rows - 8, 8), pl.ds(0, 8)))[side]
        if n == 0:
            src, dst = coefs.at[pl.ds(0, EARLY), :, at, :], wide_coefs.at[:, :, to, :]
        else:
            src, dst = source.at[:, at, :], wide_source.at[:, to, :]
        return pltpu.make_async_remote_copy(
            src_ref=src, dst_ref=dst, send_sem=side_send.at[n, side], recv_sem=side_recv.at[n, 1 - side],
            device_id=place(me - 1 if side == 0 else me + 1), device_id_type=MESH)

    pl.semaphore_wait(barrier, devices - 1)
    behind = (fluid, lax.rem(sub + subs - 1, subs))
    near = [pltpu.make_async_remote_copy(
        src_ref=src, dst_ref=dst, send_sem=near_send.at[n], recv_sem=near_recv.at[n], device_id=behind,
        device_id_type=MESH) for n, (src, dst) in enumerate(((own_pos, near_pos), (own_temp, near_temp)))]
    for copy in near:
        copy.start()
    for load in loads[:blocks]:
        load.wait()
    for c in range(CHUNKS):
        launch(0, c)
    for load in loads[blocks:]:
        load.wait()
    each(lambda side: side_copy(0, side).start())
    for l in range(EARLY):
        wide_coefs[l, :, 8 : 8 + rows, :] = coefs[l]

    lane = lax.broadcasted_iota(I32, (rows, TILE), 1)
    lower = lane < TILE // 2

    def advance(src, dst, c):
        def layer(n, _):
            l = c * deep + n
            high, low = [], []
            for zt in range(blocks):
                center = src[l + 1, zt, TOP : TOP + rows, :]
                part = center.astype(BF16)
                high.append(part)
                low.append((center - part.astype(F32)).astype(BF16))
            both = jnp.concatenate([jnp.concatenate(high, axis=0), jnp.concatenate(low, axis=0)], axis=1)
            both = dot_nn(both, weights[...])
            along = [both[zt * rows : (zt + 1) * rows, :TILE] for zt in range(blocks)]
            ends = [both[zt * rows : (zt + 1) * rows, TILE:] for zt in range(blocks)]
            nothing = jnp.zeros((rows, TILE), F32)
            for zt in range(blocks):
                end = jnp.where(lower, ends[zt - 1] if zt > 0 else nothing, ends[zt + 1] if zt + 1 < blocks else nothing)
                beside = src[l, zt, TOP : TOP + rows, :] + src[l + 2, zt, TOP : TOP + rows, :]
                beside = beside + (src[l + 1, zt, LOW : LOW + rows, :] + src[l + 1, zt, TOP + 1 : TOP + 1 + rows, :])
                beside = beside + (along[zt] + end)
                value = src[l + 1, zt, TOP : TOP + rows, :] + coefs[l, zt] * beside
                if dst is None:
                    out[l, :, zt * TILE : (zt + 1) * TILE] = value
                else:
                    dst[l + 1, zt, TOP : TOP + rows, :] = value
            return 0

        lax.fori_loop(0, deep, layer, 0, unroll=4)

    def heat_top(dst):
        for zt in range(blocks):
            dst[1, zt, TOP : TOP + rows, :] += source[zt]

    def step(k):
        src, dst = (cur, nxt) if k % 2 == 0 else (nxt, cur)

        def chunk(c, _):
            def ready():
                arrive(k, c)
                if k > 0:
                    drain(k - 1, c)

            if k == EARLY:
                pl.when(c > 0)(lambda: arrive(k, c))
                drain(k - 1, c)
            elif k == EARLY + 1:
                arrive(k, c)
                pl.when(c > 0)(lambda: drain(k - 1, c))
            else:
                ready()
            advance(src, dst, c)
            if k >= EARLY:
                pl.when(c == 0)(lambda: heat_top(dst))
            launch(k + 1, c)
            return 0

        lax.fori_loop(0, CHUNKS, chunk, 0)

    def respond(src, dst, layers_now):
        high_rows = rows + 16
        for l in range(layers_now):
            center = [src[l + 1, zt, 8 : 8 + high_rows, :] for zt in range(blocks)]
            high = [x.astype(BF16) for x in center]
            low = [(x - y.astype(F32)).astype(BF16) for x, y in zip(center, high)]
            both = jnp.concatenate([jnp.concatenate(high, axis=0), jnp.concatenate(low, axis=0)], axis=1)
            both = dot_nn(both, weights[...])
            part = [both[zt * high_rows : (zt + 1) * high_rows, :] for zt in range(blocks)]
            nothing = jnp.zeros((high_rows, TILE), F32)
            left_lanes = lax.broadcasted_iota(I32, nothing.shape, 1) < TILE // 2
            for zt in range(blocks):
                end = jnp.where(left_lanes, part[zt - 1][:, TILE:] if zt > 0 else nothing,
                                part[zt + 1][:, TILE:] if zt + 1 < blocks else nothing)
                beside = src[l, zt, 8 : 8 + high_rows, :] + src[l + 2, zt, 8 : 8 + high_rows, :]
                beside = beside + (src[l + 1, zt, 7 : 7 + high_rows, :] + src[l + 1, zt, 9 : 9 + high_rows, :])
                beside = beside + (part[zt][:, :TILE] + end)
                value = src[l + 1, zt, 8 : 8 + high_rows, :] + wide_coefs[l, zt] * beside
                dst[l + 1, zt, 8 : 8 + high_rows, :] = value + wide_source[zt] if l == 0 else value

    owners[...] = onehot(devices, row_of(owner))
    rank_row[...] = ranks(owners[...], devices)

    for copy in near:
        copy.wait_recv()
    put_features(near_pos[...], row_of(near_temp), left, None)
    for t in range(tiles):
        put_tile(left, t, tiles + t, lefts, across)

    none = jnp.zeros((32, TILE), BF16)

    def pair_group(group, _):
        for k in range(0, UNROLL, 2):
            number = group * UNROLL + k
            first = [codes[0, number + n] & (tiles - 1) for n in (0, 1)]
            second = [codes[1, number + n] & (2 * tiles - 1) for n in (0, 1)]
            stacked = jnp.concatenate([
                jnp.concatenate([rights[first[0]], none], axis=1),
                jnp.concatenate([none, rights[first[1]]], axis=1)], axis=0)
            both = dot_nn(lefts[0, second[0], :, 0:64] + lefts[1, second[1], :, 0:64], stacked)
            for n in (0, 1):
                close = jnp.maximum(both[:, n * TILE : (n + 1) * TILE], 0.0)
                gained = (close * close) * (across[second[n]] - own_temp[pl.ds(first[n], 1), :])
                at = pl.multiple_of((number + n) * 8, 8)
                partial[pl.ds(at, 8), :] = jnp.sum(gained.reshape(TILE // 8, 8, TILE), axis=0)
        return 0

    pairs = codes.shape[1]
    lax.fori_loop(0, pairs // UNROLL // 2, pair_group, 0)
    step(0)
    lax.fori_loop(pairs // UNROLL // 2, pairs // UNROLL, pair_group, 0)
    summed = partial[pl.ds(0, pairs, stride=8), :]
    for s in range(1, 8):
        summed = summed + partial[pl.ds(s, pairs, stride=8), :]
    code_row = code_rows[0:1, :]
    number = lax.broadcasted_iota(I32, code_row.shape, 1)
    first = jnp.where(number < count[0], code_row & (tiles - 1), -1)
    firsts = onehot(tiles, first)
    gain = jnp.zeros((tiles, TILE), F32)
    for part in split3(summed):
        gain = gain + dot_nn(firsts, part.astype(BF16))
    out_temp = own_temp[...] + HEAT_RATE * gain
    heated[...] = out_temp

    parts = jnp.concatenate(split3(out_temp), axis=0).T.astype(BF16)
    which_row = row_of(which)
    high = onehot(tiles, lax.shift_right_logical(which_row, 7))
    picked = dot_nn(parts, jnp.concatenate([high] * 3, axis=0))
    low = jnp.broadcast_to(which_row & (TILE - 1), picked.shape)
    hit = lax.broadcasted_iota(I32, picked.shape, 0) == low
    flux = WALL_HEAT * (jnp.sum(jnp.where(hit, picked, 0.0), axis=0, keepdims=True) - row_of(seen))
    slot = onehot(SLOTS, rank_row[...].astype(I32), F32)
    cell_row = row_of(cell)
    cells = ((cell_row & ~255).astype(F32), (cell_row & 255).astype(F32), None)
    total = jnp.zeros((devices, 2 * SLOTS), F32)
    for f, c in zip(split3(flux), cells):
        lower_half = jnp.zeros_like(slot) if c is None else slot * c
        total = total + dot_nt(owners[...], jnp.concatenate([slot * f, lower_half], axis=0).astype(BF16))
    send[...] = jnp.concatenate([total, jnp.zeros((devices, TILE - 2 * SLOTS), F32)], axis=1)

    def spread_out(src, dst, sends, recvs):
        everyone(lambda f, s: pltpu.make_async_remote_copy(
            src_ref=src.at[pl.ds(f * subs + s, 1)], dst_ref=dst.at[pl.ds(me, 1)], send_sem=sends, recv_sem=recvs,
            device_id=(f, s), device_id_type=MESH).start())
        return pltpu.make_async_remote_copy(
            src_ref=src.at[pl.ds(0, devices - 1)], dst_ref=dst.at[pl.ds(0, devices - 1)], send_sem=sends,
            recv_sem=recvs, device_id=behind, device_id_type=MESH)

    own = pltpu.make_async_copy(send.at[pl.ds(me, 1)], recv.at[pl.ds(me, 1)], own_sem.at[0])
    own.start()
    first_trip = spread_out(send, recv, first_send, first_recv)

    step(1)

    own.wait()
    first_trip.wait_recv()
    turned[...] = recv[...].T

    def place_slot(n, _):
        for k in range(4):
            s = n * 4 + k
            code = turned[pl.ds(SLOTS + s, 1), :].astype(I32)
            flux = turned[pl.ds(s, 1), :] * (1.0 / SUBSTEPS)
            at = pl.ds(pl.multiple_of(s * devices, TILE), devices)
            hot[:, at] = onehot(hot.shape[0], plate_row(code))
            low = onehot(TILE, code & (TILE - 1), F32)
            for m, part in enumerate(split2(flux)):
                lows[m * TILE : (m + 1) * TILE, at] = (low * part).astype(BF16)
        return 0

    lax.fori_loop(0, SLOTS // 4, place_slot, 0, unroll=2)
    total = dot_nt(hot[...], lows[...])
    total = total[:, :TILE] + total[:, TILE:]
    for zt in range(blocks):
        source[zt] = total[zt * rows : (zt + 1) * rows, :]
        wide_source[zt, 8 : 8 + rows, :] = total[zt * rows : (zt + 1) * rows, :]
    each(lambda side: side_copy(1, side).start())
    step(2)

    for n in (0, 1):
        each(lambda side: side_copy(n, 1 - side).wait_recv())
    for zt in range(blocks):
        resp[1, zt, 8 : 24 + rows, :] = wide_source[zt]
    pair = (resp, resp_next)
    for k in range(2, EARLY + 1):
        respond(pair[k % 2], pair[(k + 1) % 2], k)
    done = pair[(EARLY + 1) % 2]
    target = (cur, nxt)[EARLY % 2]
    arrive(EARLY, 0)
    drain(EARLY, 0)
    for l in range(EARLY):
        for zt in range(blocks):
            target[l + 1, zt, TOP : TOP + rows, :] += done[l + 1, zt, 16 : 16 + rows, :]
            target[l + 1, zt, LOW : LOW + 1, :] += done[l + 1, zt, 15:16, :]
            target[l + 1, zt, TOP + rows : TOP + rows + 1, :] += done[l + 1, zt, 16 + rows : 17 + rows, :]

    for k in range(EARLY, SUBSTEPS - 1):
        step(k)

    last = SUBSTEPS - 1
    arrive(last, 0)
    drain(last - 1, 0)
    advance(nxt, None, 0)
    for zt in range(blocks):
        out[0, :, zt * TILE : (zt + 1) * TILE] += source[zt]
    flat = jnp.concatenate([out[0, :, zt * TILE : (zt + 1) * TILE] for zt in range(blocks)], axis=0)
    wide = jnp.concatenate([flat[k : k + TILE, :].T for k in range(0, flat.shape[0], TILE)], axis=1)
    parts = jnp.concatenate(split2(wide), axis=0).astype(BF16)

    def pick_slots(n, _):
        for k in range(2):
            at = pl.ds(pl.multiple_of((n * 2 + k) * 2 * devices, TILE), 2 * devices)
            found = dot_nn(parts, hot[:, at])
            found = found[:TILE] + found[TILE:]
            s = n * 4 + k * 2
            code = jnp.concatenate([turned[pl.ds(SLOTS + s + m, 1), :] for m in (0, 1)], axis=1).astype(I32)
            low = lax.broadcasted_iota(I32, found.shape, 0) == jnp.broadcast_to(code & (TILE - 1), found.shape)
            value = jnp.sum(jnp.where(low, found, 0.0), axis=0, keepdims=True)
            for m in (0, 1):
                found_rows[pl.ds(s + m, 1), :] = value[:, m * devices : (m + 1) * devices]
        return 0

    found_rows[...] = jnp.zeros(found_rows.shape, F32)
    lax.fori_loop(0, SLOTS // 4, pick_slots, 0, unroll=2)
    values[...] = found_rows[...].T
    own = pltpu.make_async_copy(values.at[pl.ds(me, 1)], back.at[pl.ds(me, 1)], own_sem.at[1])
    own.start()
    last_trip = spread_out(values, back, last_send, last_recv)

    def closing(c, _):
        arrive(last, c)
        drain(last - 1, c)
        advance(nxt, None, c)
        return 0

    lax.fori_loop(1, CHUNKS, closing, 0)

    own.wait()
    last_trip.wait_recv()
    found = dot_nn(jnp.concatenate(split3(back[...].T[0:SLOTS, :]), axis=0).astype(BF16), owners[...])
    found = found[0:SLOTS] + found[SLOTS : 2 * SLOTS] + found[2 * SLOTS :]
    slot = onehot(SLOTS, rank_row[...].astype(I32), F32)
    ghost = jnp.sum(found * slot, axis=0, keepdims=True)
    for t in range(ghost_out.shape[0]):
        ghost_out[t : t + 1, :] = ghost[:, t * TILE : (t + 1) * TILE]

    for copy in near:
        copy.wait_send()
    first_trip.wait_send()
    last_trip.wait_send()
    for c in range(CHUNKS):
        drain(last, c)
    for n in (0, 1):
        each(lambda side: side_copy(n, side).wait_send())


def call_step(codes, count, own_pos, own_temp, which, owner, cell, seen, temp, coef, fluids, subs):
    devices = fluids * subs
    layers, rows, span = temp.shape
    blocks = span // TILE
    tiles, wide = own_temp.shape[0], own_pos.shape[1]
    ghosts = owner.shape[0] * TILE
    DMA = pltpu.SemaphoreType.DMA
    return pl.pallas_call(
        functools.partial(step_kernel, fluids, subs),
        out_shape=(
            jax.ShapeDtypeStruct(own_temp.shape, F32),
            pltpu.VMEM(temp.shape, F32),
            jax.ShapeDtypeStruct(owner.shape, F32),
        ),
        in_specs=[SMEM_SPEC] + [HBM_SPEC] * 9,
        out_specs=(VMEM_SPEC,) * 3,
        scratch_shapes=[
            pltpu.SMEM(codes.shape, I32),
            pltpu.VMEM(codes.shape, I32),
            pltpu.VMEM(own_pos.shape, F32),
            pltpu.VMEM(own_temp.shape, F32),
            pltpu.VMEM(which.shape, I32),
            pltpu.VMEM(owner.shape, I32),
            pltpu.VMEM(cell.shape, I32),
            pltpu.VMEM(seen.shape, F32),
            DMA((8,)),
            pltpu.VMEM((32, wide), F32),
            pltpu.VMEM((32, wide), F32),
            pltpu.VMEM((2, 2 * tiles, TILE, TILE), BF16),
            pltpu.VMEM((2 * tiles, TILE, TILE), F32),
            pltpu.VMEM((tiles, 32, TILE), BF16),
            pltpu.VMEM((codes.shape[1] * 8, TILE), F32),
            pltpu.VMEM(own_pos.shape, F32),
            pltpu.VMEM(own_temp.shape, F32),
            pltpu.VMEM((devices, ghosts), BF16),
            pltpu.VMEM((1, ghosts), F32),
            pltpu.VMEM((devices, TILE), F32),
            pltpu.VMEM((devices, TILE), F32),
            pltpu.VMEM((TILE, devices), F32),
            pltpu.VMEM((TILE, devices), F32),
            pltpu.VMEM((rows * blocks, devices * SLOTS), BF16),
            pltpu.VMEM((2 * TILE, devices * SLOTS), BF16),
            pltpu.VMEM((blocks, rows, TILE), F32),
            pltpu.VMEM((devices, TILE), F32),
            pltpu.VMEM((devices, TILE), F32),
            pltpu.VMEM((layers + 2, blocks, TOP + rows + 8, TILE), F32),
            pltpu.VMEM((layers + 2, blocks, TOP + rows + 8, TILE), F32),
            pltpu.VMEM((layers, blocks, rows, TILE), F32),
            pltpu.VMEM((2 * TILE, 2 * TILE), BF16),
            pltpu.VMEM((blocks, rows + 16, TILE), F32),
            pltpu.VMEM((EARLY, blocks, rows + 16, TILE), F32),
            pltpu.VMEM((EARLY + 2, blocks, rows + 32, TILE), F32),
            pltpu.VMEM((EARLY + 2, blocks, rows + 32, TILE), F32),
            DMA((2, 2)),
            DMA((2, 2)),
            DMA((2,)),
            DMA((2,)),
            DMA,
            DMA,
            DMA,
            DMA,
            DMA((2,)),
            DMA((2, blocks)),
            DMA((SUBSTEPS, 2, CHUNKS)),
            DMA((SUBSTEPS, 2, CHUNKS)),
        ],
        compiler_params=pltpu.CompilerParams(collective_id=0, has_side_effects=True, vmem_limit_bytes=48 << 20),
        name="step",
    )(count, *[pltpu.with_memory_space_constraint(x, pltpu.HBM) for x in (
        codes, own_pos, own_temp, which, owner, cell, seen, temp, coef)])


def on_device(positions, particle_temp, pair_list, pair_count, ghost_particle, ghost_owner, ghost_cell,
              wall_seen, solid_temp, conduct):
    codes = pair_list.T

    def tiled(x):
        return x.reshape(-1, TILE)

    heated, temp, ghost = call_step(
        codes, pair_count, positions, tiled(particle_temp), tiled(ghost_particle), tiled(ghost_owner),
        tiled(ghost_cell), tiled(wall_seen), solid_temp, conduct, lax.axis_size(AXES[0]), lax.axis_size(AXES[1]))
    return heated.reshape(-1), temp, ghost.reshape(-1)


def solution(mesh):
    one, rows, plate = P(AXES), P(AXES, None), P(None, AXES, None)
    return jax.shard_map(
        on_device,
        mesh=mesh,
        in_specs=(P(None, AXES), one, rows, one, one, rows, one, one, plate, plate),
        out_specs=(one, plate, one),
        check_vma=False,
    )
```

```python
import functools
import jax
import jax.numpy as jnp
from jax import lax
from jax.experimental import pallas as pl
from jax.experimental.pallas import tpu as pltpu
from jax.sharding import PartitionSpec as P

F32, BF16, I32 = jnp.float32, jnp.bfloat16, jnp.int32
TILE = 128
SUBSTEPS = 6
SLOTS = 32
HEAT_RATE = 0.004
WALL_HEAT = 0.5
UNROLL = 32
CHUNKS = 8
EARLY = 5
AXES = ("fluid", "sub")
VMEM_SPEC = pl.BlockSpec(memory_space=pltpu.VMEM)
SMEM_SPEC = pl.BlockSpec(memory_space=pltpu.SMEM)
ANY_SPEC = pl.BlockSpec(memory_space=pl.ANY)
HBM_SPEC = pl.BlockSpec(memory_space=pltpu.HBM)


def split3(x):
    high = x.astype(BF16).astype(F32)
    rest = x - high
    mid = rest.astype(BF16).astype(F32)
    return high, mid, rest - mid


def split2(x):
    high = x.astype(BF16).astype(F32)
    return high, x - high


def row_of(ref):
    return jnp.concatenate([ref[t : t + 1, :] for t in range(ref.shape[0])], axis=1)


def onehot(rows, codes, dtype=BF16):
    shape = (rows, codes.shape[1])
    hit = lax.broadcasted_iota(I32, shape, 0) == jnp.broadcast_to(codes, shape)
    return jnp.where(hit, 1.0, 0.0).astype(dtype)


def dot_nn(a, b):
    return lax.dot_general(a, b, (((1,), (0,)), ((), ())), preferred_element_type=F32)


def dot_nt(a, b):
    return lax.dot_general(a, b, (((1,), (1,)), ((), ())), preferred_element_type=F32)


def put_features(pos, temp_row, left, right):
    wide = pos.shape[1]
    moved = pos - 0.5
    high, mid, low = split3(moved)
    squares = jnp.sum(moved * moved, axis=0, keepdims=True)
    one = jnp.ones((3, wide), F32)
    minus = split3(-squares)
    temps = split3(temp_row)
    for place, part in enumerate((high, high, mid, mid, high, low)):
        left[3 * place : 3 * place + 3, :] = part
    left[18:21, :] = one
    for k in range(3):
        left[21 + k : 22 + k, :] = minus[k]
        left[24 + k : 25 + k, :] = temps[k]
    left[27:32, :] = jnp.zeros((5, wide), F32)
    if right is None:
        return
    base = split3(1.0 - squares)
    for place, part in enumerate((high, mid, high, mid, low, high)):
        right[3 * place : 3 * place + 3, :] = 2.0 * part
    for k in range(3):
        right[18 + k : 19 + k, :] = base[k]
    right[21:24, :] = one
    right[24:32, :] = jnp.zeros((8, wide), F32)


def put_tile(left, t, tile, lefts, across):
    block = left[:, t * TILE : (t + 1) * TILE]
    block = jnp.concatenate([block] * 4, axis=0).T
    lane = lax.broadcasted_iota(I32, block.shape, 1)
    lefts[0, tile] = jnp.where(lane < 32, block, 0.0).astype(BF16)
    lefts[1, tile] = jnp.where((lane >= 32) & (lane < 64), block, 0.0).astype(BF16)
    row = lax.broadcasted_iota(I32, (TILE, TILE), 0)
    take = jnp.where((row >= 24) & (row < 27), 1.0, 0.0).astype(BF16)
    across[tile] = dot_nn(lefts[0, tile], take)


def ranks(owners, devices):
    row = lax.broadcasted_iota(I32, (TILE, 2 * TILE), 0)
    col = lax.broadcasted_iota(I32, (TILE, 2 * TILE), 1)
    before = jnp.where((row < col) | (col >= TILE), 1.0, 0.0).astype(BF16)
    so_far = jnp.zeros((devices, TILE), F32)
    out = []
    for t in range(owners.shape[1] // TILE):
        mine = owners[:, t * TILE : (t + 1) * TILE]
        counted = dot_nn(mine, before)
        out.append(jnp.sum(mine.astype(F32) * (counted[:, :TILE] + so_far), axis=0, keepdims=True))
        so_far = so_far + counted[:, TILE:]
    return jnp.concatenate(out, axis=1)


def plate_row(code):
    return (lax.shift_right_logical(code, 7) & 15) * 16 + lax.shift_right_logical(code, 11)


LOW, TOP = 7, 8


def stencil_weights():
    row = lax.broadcasted_iota(I32, (2 * TILE, 2 * TILE), 0) & (TILE - 1)
    col = lax.broadcasted_iota(I32, (2 * TILE, 2 * TILE), 1)
    lane = col & (TILE - 1)
    near = jnp.where(jnp.abs(row - lane) == 1, 1.0, jnp.where(row == lane, -6.0, 0.0))
    swap = jnp.where((jnp.abs(row - lane) == TILE - 1), 1.0, 0.0)
    return jnp.where(col < TILE, near, swap).astype(BF16)


MESH = pl.DeviceIdType.MESH


def step_kernel(
    fluids, subs, count, codes_in, pos_in, temp_in, which_in, owner_in, cell_in, seen_in, temp, coef,
    heated, out, ghost_out,
    codes, code_rows, own_pos, own_temp, which, owner, cell, seen, small_sem,
    left, right, lefts, across, rights, partial, near_pos, near_temp, owners, slots, send, recv, turned, found_rows, hot, lows, source,
    values, back, cur, nxt, coefs, weights, wide_source, wide_coefs, resp, resp_next, side_send, side_recv,
    near_send, near_recv, first_send, first_recv, last_send, last_recv, own_sem, load_sem, send_sem, recv_sem,
):
    devices = fluids * subs
    layers, rows, span = temp.shape
    blocks = span // TILE
    tiles = own_temp.shape[0]
    deep = layers // CHUNKS
    fluid, sub = lax.axis_index(AXES[0]), lax.axis_index(AXES[1])
    me = fluid * subs + sub

    def place(index):
        return (lax.div(index, subs), lax.rem(index, subs))

    def everyone(act):
        half = fluids // 2

        def row(up, _):
            other = lax.rem(fluid + 1 + lax.rem(up + half, fluids - 1), fluids)
            for by in range(subs):
                act(other, lax.rem(sub + subs // 2 + by, subs))
            return 0

        lax.fori_loop(0, fluids - 1, row, 0)
        for by in range(1, subs):
            act(fluid, lax.rem(sub + by, subs))

    small = [pltpu.make_async_copy(src, dst, small_sem.at[n]) for n, (src, dst) in enumerate((
        (codes_in, codes), (codes_in, code_rows), (pos_in, own_pos), (temp_in, own_temp), (which_in, which),
        (owner_in, owner), (cell_in, cell), (seen_in, seen)))]
    for copy in small:
        copy.start()

    loads = []
    for array, buf, offset in ((temp, cur, 1), (coef, coefs, 0)):
        for zt in range(blocks):
            at = pl.ds(zt * TILE, TILE)
            where = pl.ds(TOP, rows) if offset else pl.ds(0, rows)
            loads.append(pltpu.make_async_copy(
                array.at[:, :, at], buf.at[pl.ds(offset, layers), zt, where, :], load_sem.at[1 - offset, zt]))
    for load in loads:
        load.start()

    barrier = pltpu.get_barrier_semaphore()
    everyone(lambda f, s: pl.semaphore_signal(barrier, inc=1, device_id=(f, s), device_id_type=MESH))

    weights[...] = stencil_weights()
    for l in (0, layers + 1):
        for buf in (cur, nxt):
            for zt in range(blocks):
                buf[l, zt, TOP : TOP + rows, :] = jnp.zeros((rows, TILE), F32)

    for buf in (resp, resp_next):
        buf[...] = jnp.zeros(buf.shape, F32)

    for edge, x, far in ((0, LOW, 0), (devices - 1, TOP + rows, rows + 8)):
        @pl.when(me == edge)
        def _():
            wide_source[:, far : far + 8, :] = jnp.zeros((blocks, 8, TILE), F32)
            wide_coefs[:, :, far : far + 8, :] = jnp.zeros((EARLY, blocks, 8, TILE), F32)

            def wipe(l, _):
                for buf in (cur, nxt):
                    for zt in range(blocks):
                        buf[l, zt, x : x + 1, :] = jnp.zeros((1, TILE), F32)
                return 0

            lax.fori_loop(1, layers + 1, wipe, 0)

    for copy in small:
        copy.wait()
    put_features(own_pos[...], row_of(own_temp), left, right)
    for t in range(tiles):
        put_tile(left, t, t, lefts, across)
        rights[t] = right[:, t * TILE : (t + 1) * TILE].astype(BF16)

    def halo(k, side, c):
        buf = (cur, nxt)[k % 2]
        x, y = ((TOP, TOP + rows), (TOP + rows - 1, LOW))[side]
        at = pl.ds(1 + c * deep, deep)
        return pltpu.make_async_remote_copy(
            src_ref=buf.at[at, :, pl.ds(x, 1), :], dst_ref=buf.at[at, :, pl.ds(y, 1), :],
            send_sem=send_sem.at[k, side, c], recv_sem=recv_sem.at[k, 1 - side, c],
            device_id=place(me - 1 if side == 0 else me + 1), device_id_type=MESH)

    has = (me > 0, me < devices - 1)

    def each(act):
        for side in (0, 1):
            @pl.when(has[side])
            def _():
                act(side)

    def launch(k, c):
        each(lambda side: halo(k, side, c).start())

    def arrive(k, c):
        each(lambda side: halo(k, 1 - side, c).wait_recv())

    def drain(k, c):
        each(lambda side: halo(k, side, c).wait_send())

    def side_copy(n, side):
        at, to = ((pl.ds(0, 8), pl.ds(rows + 8, 8)), (pl.ds(rows - 8, 8), pl.ds(0, 8)))[side]
        if n == 0:
            src, dst = coefs.at[pl.ds(0, EARLY), :, at, :], wide_coefs.at[:, :, to, :]
        else:
            src, dst = source.at[:, at, :], wide_source.at[:, to, :]
        return pltpu.make_async_remote_copy(
            src_ref=src, dst_ref=dst, send_sem=side_send.at[n, side], recv_sem=side_recv.at[n, 1 - side],
            device_id=place(me - 1 if side == 0 else me + 1), device_id_type=MESH)

    pl.semaphore_wait(barrier, devices - 1)
    behind = (fluid, lax.rem(sub + subs - 1, subs))
    near = [pltpu.make_async_remote_copy(
        src_ref=src, dst_ref=dst, send_sem=near_send.at[n], recv_sem=near_recv.at[n], device_id=behind,
        device_id_type=MESH) for n, (src, dst) in enumerate(((own_pos, near_pos), (own_temp, near_temp)))]
    for copy in near:
        copy.start()
    for load in loads[:blocks]:
        load.wait()
    for c in range(CHUNKS):
        launch(0, c)
    for load in loads[blocks:]:
        load.wait()
    each(lambda side: side_copy(0, side).start())
    for l in range(EARLY):
        wide_coefs[l, :, 8 : 8 + rows, :] = coefs[l]

    lane = lax.broadcasted_iota(I32, (rows, TILE), 1)
    lower = lane < TILE // 2

    def advance(src, dst, c):
        def layer(n, _):
            l = c * deep + n
            high, low = [], []
            for zt in range(blocks):
                center = src[l + 1, zt, TOP : TOP + rows, :]
                part = center.astype(BF16)
                high.append(part)
                low.append((center - part.astype(F32)).astype(BF16))
            both = jnp.concatenate([jnp.concatenate(high, axis=0), jnp.concatenate(low, axis=0)], axis=1)
            both = dot_nn(both, weights[...])
            along = [both[zt * rows : (zt + 1) * rows, :TILE] for zt in range(blocks)]
            ends = [both[zt * rows : (zt + 1) * rows, TILE:] for zt in range(blocks)]
            nothing = jnp.zeros((rows, TILE), F32)
            for zt in range(blocks):
                end = jnp.where(lower, ends[zt - 1] if zt > 0 else nothing, ends[zt + 1] if zt + 1 < blocks else nothing)
                beside = src[l, zt, TOP : TOP + rows, :] + src[l + 2, zt, TOP : TOP + rows, :]
                beside = beside + (src[l + 1, zt, LOW : LOW + rows, :] + src[l + 1, zt, TOP + 1 : TOP + 1 + rows, :])
                beside = beside + (along[zt] + end)
                value = src[l + 1, zt, TOP : TOP + rows, :] + coefs[l, zt] * beside
                if dst is None:
                    out[l, :, zt * TILE : (zt + 1) * TILE] = value
                else:
                    dst[l + 1, zt, TOP : TOP + rows, :] = value
            return 0

        lax.fori_loop(0, deep, layer, 0, unroll=4)

    def step(k, first=0, end=CHUNKS):
        src, dst = (cur, nxt) if k % 2 == 0 else (nxt, cur)

        def chunk(c, _):
            arrive(k, c)
            if k > 0:
                drain(k - 1, c)
            advance(src, dst, c)
            launch(k + 1, c)
            return 0

        lax.fori_loop(first, end, chunk, 0)

    def respond(src, dst, layers_now):
        high_rows = rows + 16
        for l in range(layers_now):
            center = [src[l + 1, zt, 8 : 8 + high_rows, :] for zt in range(blocks)]
            high = [x.astype(BF16) for x in center]
            low = [(x - y.astype(F32)).astype(BF16) for x, y in zip(center, high)]
            both = jnp.concatenate([jnp.concatenate(high, axis=0), jnp.concatenate(low, axis=0)], axis=1)
            both = dot_nn(both, weights[...])
            part = [both[zt * high_rows : (zt + 1) * high_rows, :] for zt in range(blocks)]
            nothing = jnp.zeros((high_rows, TILE), F32)
            left_lanes = lax.broadcasted_iota(I32, nothing.shape, 1) < TILE // 2
            for zt in range(blocks):
                end = jnp.where(left_lanes, part[zt - 1][:, TILE:] if zt > 0 else nothing,
                                part[zt + 1][:, TILE:] if zt + 1 < blocks else nothing)
                beside = src[l, zt, 8 : 8 + high_rows, :] + src[l + 2, zt, 8 : 8 + high_rows, :]
                beside = beside + (src[l + 1, zt, 7 : 7 + high_rows, :] + src[l + 1, zt, 9 : 9 + high_rows, :])
                beside = beside + (part[zt][:, :TILE] + end)
                value = src[l + 1, zt, 8 : 8 + high_rows, :] + wide_coefs[l, zt] * beside
                dst[l + 1, zt, 8 : 8 + high_rows, :] = value + wide_source[zt] if l == 0 else value

    owners[...] = onehot(devices, row_of(owner))
    slots[...] = onehot(SLOTS, ranks(owners[...], devices).astype(I32), F32)

    for copy in near:
        copy.wait_recv()
    put_features(near_pos[...], row_of(near_temp), left, None)
    for t in range(tiles):
        put_tile(left, t, tiles + t, lefts, across)

    none = jnp.zeros((32, TILE), BF16)

    def pair_group(group, _):
        for k in range(0, UNROLL, 2):
            number = group * UNROLL + k
            first = [codes[0, number + n] & (tiles - 1) for n in (0, 1)]
            second = [codes[1, number + n] & (2 * tiles - 1) for n in (0, 1)]
            stacked = jnp.concatenate([
                jnp.concatenate([rights[first[0]], none], axis=1),
                jnp.concatenate([none, rights[first[1]]], axis=1)], axis=0)
            both = dot_nn(lefts[0, second[0], :, 0:64] + lefts[1, second[1], :, 0:64], stacked)
            for n in (0, 1):
                close = jnp.maximum(both[:, n * TILE : (n + 1) * TILE], 0.0)
                gained = (close * close) * (across[second[n]] - own_temp[pl.ds(first[n], 1), :])
                at = pl.multiple_of((number + n) * 8, 8)
                partial[pl.ds(at, 8), :] = jnp.sum(gained.reshape(TILE // 8, 8, TILE), axis=0)
        return 0

    pairs = codes.shape[1]
    lax.fori_loop(0, pairs // UNROLL // 2, pair_group, 0)
    step(0)
    lax.fori_loop(pairs // UNROLL // 2, pairs // UNROLL, pair_group, 0)
    step(1)
    summed = partial[pl.ds(0, pairs, stride=8), :]
    for s in range(1, 8):
        summed = summed + partial[pl.ds(s, pairs, stride=8), :]
    code_row = code_rows[0:1, :]
    number = lax.broadcasted_iota(I32, code_row.shape, 1)
    first = jnp.where(number < count[0], code_row & (tiles - 1), -1)
    firsts = onehot(tiles, first)
    gain = jnp.zeros((tiles, TILE), F32)
    for part in split3(summed):
        gain = gain + dot_nn(firsts, part.astype(BF16))
    out_temp = own_temp[...] + HEAT_RATE * gain
    heated[...] = out_temp

    parts = jnp.concatenate(split3(out_temp), axis=0).T.astype(BF16)
    which_row = row_of(which)
    high = onehot(tiles, lax.shift_right_logical(which_row, 7))
    picked = dot_nn(parts, jnp.concatenate([high] * 3, axis=0))
    low = jnp.broadcast_to(which_row & (TILE - 1), picked.shape)
    hit = lax.broadcasted_iota(I32, picked.shape, 0) == low
    flux = WALL_HEAT * (jnp.sum(jnp.where(hit, picked, 0.0), axis=0, keepdims=True) - row_of(seen))
    slot = slots[...]
    cell_row = row_of(cell)
    cells = ((cell_row & ~255).astype(F32), (cell_row & 255).astype(F32), None)
    total = jnp.zeros((devices, 2 * SLOTS), F32)
    for f, c in zip(split3(flux), cells):
        lower_half = jnp.zeros_like(slot) if c is None else slot * c
        total = total + dot_nt(owners[...], jnp.concatenate([slot * f, lower_half], axis=0).astype(BF16))
    send[...] = jnp.concatenate([total, jnp.zeros((devices, TILE - 2 * SLOTS), F32)], axis=1)

    def spread_out(src, dst, sends, recvs):
        everyone(lambda f, s: pltpu.make_async_remote_copy(
            src_ref=src.at[pl.ds(f * subs + s, 1)], dst_ref=dst.at[pl.ds(me, 1)], send_sem=sends, recv_sem=recvs,
            device_id=(f, s), device_id_type=MESH).start())
        return pltpu.make_async_remote_copy(
            src_ref=src.at[pl.ds(0, devices - 1)], dst_ref=dst.at[pl.ds(0, devices - 1)], send_sem=sends,
            recv_sem=recvs, device_id=behind, device_id_type=MESH)

    own = pltpu.make_async_copy(send.at[pl.ds(me, 1)], recv.at[pl.ds(me, 1)], own_sem.at[0])
    own.start()
    first_trip = spread_out(send, recv, first_send, first_recv)

    step(2)

    own.wait()
    first_trip.wait_recv()
    turned[...] = recv[...].T

    def place_slot(n, _):
        for k in range(4):
            s = n * 4 + k
            code = turned[pl.ds(SLOTS + s, 1), :].astype(I32)
            flux = turned[pl.ds(s, 1), :] * (1.0 / SUBSTEPS)
            at = pl.ds(pl.multiple_of(s * devices, TILE), devices)
            hot[:, at] = onehot(hot.shape[0], plate_row(code))
            low = onehot(TILE, code & (TILE - 1), F32)
            for m, part in enumerate(split2(flux)):
                lows[m * TILE : (m + 1) * TILE, at] = (low * part).astype(BF16)
        return 0

    lax.fori_loop(0, SLOTS // 4, place_slot, 0, unroll=2)
    total = dot_nt(hot[...], lows[...])
    total = total[:, :TILE] + total[:, TILE:]
    for zt in range(blocks):
        source[zt] = total[zt * rows : (zt + 1) * rows, :]
        wide_source[zt, 8 : 8 + rows, :] = total[zt * rows : (zt + 1) * rows, :]
    each(lambda side: side_copy(1, side).start())
    step(3)
    ahead = 2
    step(4, 0, ahead)

    for n in (0, 1):
        each(lambda side: side_copy(n, 1 - side).wait_recv())
    for zt in range(blocks):
        resp[1, zt, 8 : 24 + rows, :] = wide_source[zt]
    pair = (resp, resp_next)
    for k in range(2, EARLY + 1):
        respond(pair[k % 2], pair[(k + 1) % 2], k)
    done = pair[(EARLY + 1) % 2]
    target = (cur, nxt)[EARLY % 2]
    for c in range(ahead):
        arrive(EARLY, c)
        drain(EARLY, c)
    for l in range(EARLY):
        for zt in range(blocks):
            target[l + 1, zt, TOP : TOP + rows, :] += done[l + 1, zt, 16 : 16 + rows, :]
            target[l + 1, zt, LOW : LOW + 1, :] += done[l + 1, zt, 15:16, :]
            target[l + 1, zt, TOP + rows : TOP + rows + 1, :] += done[l + 1, zt, 16 + rows : 17 + rows, :]

    last = SUBSTEPS - 1
    advance(nxt, None, 0)
    for zt in range(blocks):
        out[0, :, zt * TILE : (zt + 1) * TILE] += source[zt]
    flat = jnp.concatenate([out[0, :, zt * TILE : (zt + 1) * TILE] for zt in range(blocks)], axis=0)
    wide = jnp.concatenate([flat[k : k + TILE, :].T for k in range(0, flat.shape[0], TILE)], axis=1)
    parts = jnp.concatenate(split2(wide), axis=0).astype(BF16)

    def pick_slots(n, _):
        for k in range(2):
            at = pl.ds(pl.multiple_of((n * 2 + k) * 2 * devices, TILE), 2 * devices)
            found = dot_nn(parts, hot[:, at])
            found = found[:TILE] + found[TILE:]
            s = n * 4 + k * 2
            code = jnp.concatenate([turned[pl.ds(SLOTS + s + m, 1), :] for m in (0, 1)], axis=1).astype(I32)
            low = lax.broadcasted_iota(I32, found.shape, 0) == jnp.broadcast_to(code & (TILE - 1), found.shape)
            value = jnp.sum(jnp.where(low, found, 0.0), axis=0, keepdims=True)
            for m in (0, 1):
                found_rows[pl.ds(s + m, 1), :] = value[:, m * devices : (m + 1) * devices]
        return 0

    found_rows[...] = jnp.zeros(found_rows.shape, F32)
    lax.fori_loop(0, SLOTS // 4, pick_slots, 0, unroll=2)
    values[...] = found_rows[...].T
    own = pltpu.make_async_copy(values.at[pl.ds(me, 1)], back.at[pl.ds(me, 1)], own_sem.at[1])
    own.start()
    last_trip = spread_out(values, back, last_send, last_recv)
    step(4, ahead, CHUNKS)

    def closing(c, _):
        pl.when(c >= ahead)(lambda: arrive(last, c))
        advance(nxt, None, c)
        return 0

    lax.fori_loop(1, CHUNKS, closing, 0)

    own.wait()
    last_trip.wait_recv()
    found = dot_nn(jnp.concatenate(split2(back[...].T[0:SLOTS, :]), axis=0).astype(BF16), owners[...])
    ghost = jnp.sum((found[0:SLOTS] + found[SLOTS:]) * slots[...], axis=0, keepdims=True)
    for t in range(ghost_out.shape[0]):
        ghost_out[t : t + 1, :] = ghost[:, t * TILE : (t + 1) * TILE]

    for copy in near:
        copy.wait_send()
    first_trip.wait_send()
    last_trip.wait_send()
    for c in range(CHUNKS):
        drain(last - 1, c)
        if c >= ahead:
            drain(last, c)
    for n in (0, 1):
        each(lambda side: side_copy(n, side).wait_send())


def call_step(codes, count, own_pos, own_temp, which, owner, cell, seen, temp, coef, fluids, subs):
    devices = fluids * subs
    layers, rows, span = temp.shape
    blocks = span // TILE
    tiles, wide = own_temp.shape[0], own_pos.shape[1]
    ghosts = owner.shape[0] * TILE
    DMA = pltpu.SemaphoreType.DMA
    return pl.pallas_call(
        functools.partial(step_kernel, fluids, subs),
        out_shape=(
            pltpu.VMEM(own_temp.shape, F32),
            pltpu.VMEM(temp.shape, F32),
            pltpu.VMEM(owner.shape, F32),
        ),
        in_specs=[SMEM_SPEC] + [HBM_SPEC] * 9,
        out_specs=(VMEM_SPEC,) * 3,
        scratch_shapes=[
            pltpu.SMEM(codes.shape, I32),
            pltpu.VMEM(codes.shape, I32),
            pltpu.VMEM(own_pos.shape, F32),
            pltpu.VMEM(own_temp.shape, F32),
            pltpu.VMEM(which.shape, I32),
            pltpu.VMEM(owner.shape, I32),
            pltpu.VMEM(cell.shape, I32),
            pltpu.VMEM(seen.shape, F32),
            DMA((8,)),
            pltpu.VMEM((32, wide), F32),
            pltpu.VMEM((32, wide), F32),
            pltpu.VMEM((2, 2 * tiles, TILE, TILE), BF16),
            pltpu.VMEM((2 * tiles, TILE, TILE), F32),
            pltpu.VMEM((tiles, 32, TILE), BF16),
            pltpu.VMEM((codes.shape[1] * 8, TILE), F32),
            pltpu.VMEM(own_pos.shape, F32),
            pltpu.VMEM(own_temp.shape, F32),
            pltpu.VMEM((devices, ghosts), BF16),
            pltpu.VMEM((SLOTS, ghosts), F32),
            pltpu.VMEM((devices, TILE), F32),
            pltpu.VMEM((devices, TILE), F32),
            pltpu.VMEM((TILE, devices), F32),
            pltpu.VMEM((TILE, devices), F32),
            pltpu.VMEM((rows * blocks, devices * SLOTS), BF16),
            pltpu.VMEM((2 * TILE, devices * SLOTS), BF16),
            pltpu.VMEM((blocks, rows, TILE), F32),
            pltpu.VMEM((devices, TILE), F32),
            pltpu.VMEM((devices, TILE), F32),
            pltpu.VMEM((layers + 2, blocks, TOP + rows + 8, TILE), F32),
            pltpu.VMEM((layers + 2, blocks, TOP + rows + 8, TILE), F32),
            pltpu.VMEM((layers, blocks, rows, TILE), F32),
            pltpu.VMEM((2 * TILE, 2 * TILE), BF16),
            pltpu.VMEM((blocks, rows + 16, TILE), F32),
            pltpu.VMEM((EARLY, blocks, rows + 16, TILE), F32),
            pltpu.VMEM((EARLY + 2, blocks, rows + 32, TILE), F32),
            pltpu.VMEM((EARLY + 2, blocks, rows + 32, TILE), F32),
            DMA((2, 2)),
            DMA((2, 2)),
            DMA((2,)),
            DMA((2,)),
            DMA,
            DMA,
            DMA,
            DMA,
            DMA((2,)),
            DMA((2, blocks)),
            DMA((SUBSTEPS, 2, CHUNKS)),
            DMA((SUBSTEPS, 2, CHUNKS)),
        ],
        compiler_params=pltpu.CompilerParams(collective_id=0, has_side_effects=True, vmem_limit_bytes=48 << 20),
        name="step",
    )(count, *[pltpu.with_memory_space_constraint(x, pltpu.HBM) for x in (
        codes, own_pos, own_temp, which, owner, cell, seen, temp, coef)])


def finish_kernel(plate, first, second, plate_out, first_out, second_out, sem):
    deep = plate.shape[0] // 8
    copies = [pltpu.make_async_copy(plate.at[pl.ds(n * deep, deep)], plate_out.at[pl.ds(n * deep, deep)], sem.at[n]) for n in range(8)]
    copies.append(pltpu.make_async_copy(first, first_out, sem.at[8]))
    copies.append(pltpu.make_async_copy(second, second_out, sem.at[9]))
    for copy in copies:
        copy.start()
    for copy in copies:
        copy.wait()


def call_finish(*arrays):
    return pl.pallas_call(
        finish_kernel,
        out_shape=tuple(jax.ShapeDtypeStruct(x.shape, x.dtype) for x in arrays),
        in_specs=[VMEM_SPEC] * 3,
        out_specs=(HBM_SPEC,) * 3,
        scratch_shapes=[pltpu.SemaphoreType.DMA((10,))],
        compiler_params=pltpu.CompilerParams(vmem_limit_bytes=16 << 20),
        name="finish",
    )(*arrays)


def on_device(positions, particle_temp, pair_list, pair_count, ghost_particle, ghost_owner, ghost_cell,
              wall_seen, solid_temp, conduct):
    codes = pair_list.T

    def tiled(x):
        return x.reshape(-1, TILE)

    heated, temp, ghost = call_step(
        codes, pair_count, positions, tiled(particle_temp), tiled(ghost_particle), tiled(ghost_owner),
        tiled(ghost_cell), tiled(wall_seen), solid_temp, conduct, lax.axis_size(AXES[0]), lax.axis_size(AXES[1]))
    temp, heated, ghost = call_finish(temp, heated, ghost)
    return heated.reshape(-1), temp, ghost.reshape(-1)


def solution(mesh):
    one, rows, plate = P(AXES), P(AXES, None), P(None, AXES, None)
    return jax.shard_map(
        on_device,
        mesh=mesh,
        in_specs=(P(None, AXES), one, rows, one, one, rows, one, one, plate, plate),
        out_specs=(one, plate, one),
        check_vma=False,
    )
```

```python
import functools
import jax
import jax.numpy as jnp
from jax import lax
from jax.experimental import pallas as pl
from jax.experimental.pallas import tpu as pltpu
from jax.sharding import PartitionSpec as P

F32, BF16, I32 = jnp.float32, jnp.bfloat16, jnp.int32
TILE = 128
SUBSTEPS = 6
SLOTS = 32
HEAT_RATE = 0.004
WALL_HEAT = 0.5
UNROLL = 32
CHUNKS = 8
EARLY = 5
AXES = ("fluid", "sub")
VMEM_SPEC = pl.BlockSpec(memory_space=pltpu.VMEM)
SMEM_SPEC = pl.BlockSpec(memory_space=pltpu.SMEM)
ANY_SPEC = pl.BlockSpec(memory_space=pl.ANY)
HBM_SPEC = pl.BlockSpec(memory_space=pltpu.HBM)


def split3(x):
    high = x.astype(BF16).astype(F32)
    rest = x - high
    mid = rest.astype(BF16).astype(F32)
    return high, mid, rest - mid


def split2(x):
    high = x.astype(BF16).astype(F32)
    return high, x - high


def row_of(ref):
    return jnp.concatenate([ref[t : t + 1, :] for t in range(ref.shape[0])], axis=1)


def onehot(rows, codes, dtype=BF16):
    shape = (rows, codes.shape[1])
    hit = lax.broadcasted_iota(I32, shape, 0) == jnp.broadcast_to(codes, shape)
    return jnp.where(hit, 1.0, 0.0).astype(dtype)


def dot_nn(a, b):
    return lax.dot_general(a, b, (((1,), (0,)), ((), ())), preferred_element_type=F32)


def dot_nt(a, b):
    return lax.dot_general(a, b, (((1,), (1,)), ((), ())), preferred_element_type=F32)


def put_features(pos, temp_row, left, right):
    wide = pos.shape[1]
    moved = pos - 0.5
    high, mid, low = split3(moved)
    squares = jnp.sum(moved * moved, axis=0, keepdims=True)
    one = jnp.ones((3, wide), F32)
    minus = split3(-squares)
    temps = split3(temp_row)
    for place, part in enumerate((high, high, mid, mid, high, low)):
        left[3 * place : 3 * place + 3, :] = part
    left[18:21, :] = one
    for k in range(3):
        left[21 + k : 22 + k, :] = minus[k]
        left[24 + k : 25 + k, :] = temps[k]
    left[27:32, :] = jnp.zeros((5, wide), F32)
    if right is None:
        return
    base = split3(1.0 - squares)
    for place, part in enumerate((high, mid, high, mid, low, high)):
        right[3 * place : 3 * place + 3, :] = 2.0 * part
    for k in range(3):
        right[18 + k : 19 + k, :] = base[k]
    right[21:24, :] = one
    right[24:32, :] = jnp.zeros((8, wide), F32)


def put_tile(left, t, tile, lefts, across):
    block = left[:, t * TILE : (t + 1) * TILE]
    block = jnp.concatenate([block] * 4, axis=0).T
    lane = lax.broadcasted_iota(I32, block.shape, 1)
    lefts[0, tile] = jnp.where(lane < 32, block, 0.0).astype(BF16)
    lefts[1, tile] = jnp.where((lane >= 32) & (lane < 64), block, 0.0).astype(BF16)
    row = lax.broadcasted_iota(I32, (TILE, TILE), 0)
    take = jnp.where((row >= 24) & (row < 27), 1.0, 0.0).astype(BF16)
    across[tile] = dot_nn(lefts[0, tile], take)


def ranks(owners, devices):
    row = lax.broadcasted_iota(I32, (TILE, 2 * TILE), 0)
    col = lax.broadcasted_iota(I32, (TILE, 2 * TILE), 1)
    before = jnp.where((row < col) | (col >= TILE), 1.0, 0.0).astype(BF16)
    so_far = jnp.zeros((devices, TILE), F32)
    out = []
    for t in range(owners.shape[1] // TILE):
        mine = owners[:, t * TILE : (t + 1) * TILE]
        counted = dot_nn(mine, before)
        out.append(jnp.sum(mine.astype(F32) * (counted[:, :TILE] + so_far), axis=0, keepdims=True))
        so_far = so_far + counted[:, TILE:]
    return jnp.concatenate(out, axis=1)


def plate_row(code):
    return (lax.shift_right_logical(code, 7) & 15) * 16 + lax.shift_right_logical(code, 11)


LOW, TOP = 7, 8


def stencil_weights():
    row = lax.broadcasted_iota(I32, (2 * TILE, 2 * TILE), 0) & (TILE - 1)
    col = lax.broadcasted_iota(I32, (2 * TILE, 2 * TILE), 1)
    lane = col & (TILE - 1)
    near = jnp.where(jnp.abs(row - lane) == 1, 1.0, jnp.where(row == lane, -6.0, 0.0))
    swap = jnp.where((jnp.abs(row - lane) == TILE - 1), 1.0, 0.0)
    return jnp.where(col < TILE, near, swap).astype(BF16)


MESH = pl.DeviceIdType.MESH


def step_kernel(
    fluids, subs, count, codes_in, pos_in, temp_in, which_in, owner_in, cell_in, seen_in, temp, coef,
    heated, out, ghost_out,
    codes, code_rows, own_pos, own_temp, which, owner, cell, seen, small_sem,
    left, right, lefts, across, rights, partial, near_pos, near_temp, owners, slots, send, recv, turned, found_rows, hot, lows, source,
    values, back, cur, nxt, coefs, weights, wide_source, wide_coefs, resp, resp_next, side_send, side_recv,
    near_send, near_recv, first_send, first_recv, last_send, last_recv, own_sem, load_sem, send_sem, recv_sem,
):
    devices = fluids * subs
    layers, rows, span = temp.shape
    blocks = span // TILE
    tiles = own_temp.shape[0]
    deep = layers // CHUNKS
    fluid, sub = lax.axis_index(AXES[0]), lax.axis_index(AXES[1])
    me = fluid * subs + sub

    def place(index):
        return (lax.div(index, subs), lax.rem(index, subs))

    def everyone(act):
        half = fluids // 2

        def row(up, _):
            other = lax.rem(fluid + 1 + lax.rem(up + half, fluids - 1), fluids)
            for by in range(subs):
                act(other, lax.rem(sub + subs // 2 + by, subs))
            return 0

        lax.fori_loop(0, fluids - 1, row, 0)
        for by in range(1, subs):
            act(fluid, lax.rem(sub + by, subs))

    small = [pltpu.make_async_copy(src, dst, small_sem.at[n]) for n, (src, dst) in enumerate((
        (codes_in, codes), (codes_in, code_rows), (pos_in, own_pos), (temp_in, own_temp), (which_in, which),
        (owner_in, owner), (cell_in, cell), (seen_in, seen)))]
    for copy in small:
        copy.start()

    loads = []
    for array, buf, offset in ((temp, cur, 1), (coef, coefs, 0)):
        for zt in range(blocks):
            at = pl.ds(zt * TILE, TILE)
            where = pl.ds(TOP, rows) if offset else pl.ds(0, rows)
            loads.append(pltpu.make_async_copy(
                array.at[:, :, at], buf.at[pl.ds(offset, layers), zt, where, :], load_sem.at[1 - offset, zt]))
    for load in loads:
        load.start()

    barrier = pltpu.get_barrier_semaphore()
    everyone(lambda f, s: pl.semaphore_signal(barrier, inc=1, device_id=(f, s), device_id_type=MESH))

    weights[...] = stencil_weights()
    for l in (0, layers + 1):
        for buf in (cur, nxt):
            for zt in range(blocks):
                buf[l, zt, TOP : TOP + rows, :] = jnp.zeros((rows, TILE), F32)

    for buf in (resp, resp_next):
        buf[...] = jnp.zeros(buf.shape, F32)

    for edge, x, far in ((0, LOW, 0), (devices - 1, TOP + rows, rows + 8)):
        @pl.when(me == edge)
        def _():
            wide_source[:, far : far + 8, :] = jnp.zeros((blocks, 8, TILE), F32)
            wide_coefs[:, :, far : far + 8, :] = jnp.zeros((EARLY, blocks, 8, TILE), F32)

            def wipe(l, _):
                for buf in (cur, nxt):
                    for zt in range(blocks):
                        buf[l, zt, x : x + 1, :] = jnp.zeros((1, TILE), F32)
                return 0

            lax.fori_loop(1, layers + 1, wipe, 0)

    for copy in small:
        copy.wait()
    put_features(own_pos[...], row_of(own_temp), left, right)
    for t in range(tiles):
        put_tile(left, t, t, lefts, across)
        rights[t] = right[:, t * TILE : (t + 1) * TILE].astype(BF16)

    def halo(k, side, c):
        buf = (cur, nxt)[k % 2]
        x, y = ((TOP, TOP + rows), (TOP + rows - 1, LOW))[side]
        at = pl.ds(1 + c * deep, deep)
        return pltpu.make_async_remote_copy(
            src_ref=buf.at[at, :, pl.ds(x, 1), :], dst_ref=buf.at[at, :, pl.ds(y, 1), :],
            send_sem=send_sem.at[k, side, c], recv_sem=recv_sem.at[k, 1 - side, c],
            device_id=place(me - 1 if side == 0 else me + 1), device_id_type=MESH)

    has = (me > 0, me < devices - 1)

    def each(act):
        for side in (0, 1):
            @pl.when(has[side])
            def _():
                act(side)

    def launch(k, c):
        each(lambda side: halo(k, side, c).start())

    def arrive(k, c):
        each(lambda side: halo(k, 1 - side, c).wait_recv())

    def drain(k, c):
        each(lambda side: halo(k, side, c).wait_send())

    def side_copy(n, side):
        at, to = ((pl.ds(0, 8), pl.ds(rows + 8, 8)), (pl.ds(rows - 8, 8), pl.ds(0, 8)))[side]
        if n == 0:
            src, dst = coefs.at[pl.ds(0, EARLY), :, at, :], wide_coefs.at[:, :, to, :]
        else:
            src, dst = source.at[:, at, :], wide_source.at[:, to, :]
        return pltpu.make_async_remote_copy(
            src_ref=src, dst_ref=dst, send_sem=side_send.at[n, side], recv_sem=side_recv.at[n, 1 - side],
            device_id=place(me - 1 if side == 0 else me + 1), device_id_type=MESH)

    pl.semaphore_wait(barrier, devices - 1)
    behind = (fluid, lax.rem(sub + subs - 1, subs))
    near = [pltpu.make_async_remote_copy(
        src_ref=src, dst_ref=dst, send_sem=near_send.at[n], recv_sem=near_recv.at[n], device_id=behind,
        device_id_type=MESH) for n, (src, dst) in enumerate(((own_pos, near_pos), (own_temp, near_temp)))]
    for copy in near:
        copy.start()
    for load in loads[:blocks]:
        load.wait()
    for c in range(CHUNKS):
        launch(0, c)
    for load in loads[blocks:]:
        load.wait()
    each(lambda side: side_copy(0, side).start())
    for l in range(EARLY):
        wide_coefs[l, :, 8 : 8 + rows, :] = coefs[l]

    lane = lax.broadcasted_iota(I32, (rows, TILE), 1)
    lower = lane < TILE // 2

    def advance(src, dst, c):
        def layer(n, _):
            l = c * deep + n
            high, low = [], []
            for zt in range(blocks):
                center = src[l + 1, zt, TOP : TOP + rows, :]
                part = center.astype(BF16)
                high.append(part)
                low.append((center - part.astype(F32)).astype(BF16))
            both = jnp.concatenate([jnp.concatenate(high, axis=0), jnp.concatenate(low, axis=0)], axis=1)
            both = dot_nn(both, weights[...])
            along = [both[zt * rows : (zt + 1) * rows, :TILE] for zt in range(blocks)]
            ends = [both[zt * rows : (zt + 1) * rows, TILE:] for zt in range(blocks)]
            nothing = jnp.zeros((rows, TILE), F32)
            for zt in range(blocks):
                end = jnp.where(lower, ends[zt - 1] if zt > 0 else nothing, ends[zt + 1] if zt + 1 < blocks else nothing)
                beside = src[l, zt, TOP : TOP + rows, :] + src[l + 2, zt, TOP : TOP + rows, :]
                beside = beside + (src[l + 1, zt, LOW : LOW + rows, :] + src[l + 1, zt, TOP + 1 : TOP + 1 + rows, :])
                beside = beside + (along[zt] + end)
                value = src[l + 1, zt, TOP : TOP + rows, :] + coefs[l, zt] * beside
                if dst is None:
                    out[l, :, zt * TILE : (zt + 1) * TILE] = value
                else:
                    dst[l + 1, zt, TOP : TOP + rows, :] = value
            return 0

        lax.fori_loop(0, deep, layer, 0, unroll=4)

    def step(k, first=0, end=CHUNKS):
        src, dst = (cur, nxt) if k % 2 == 0 else (nxt, cur)

        def chunk(c, _):
            arrive(k, c)
            if k > 0:
                drain(k - 1, c)
            advance(src, dst, c)
            launch(k + 1, c)
            return 0

        lax.fori_loop(first, end, chunk, 0)

    def respond(src, dst, layers_now):
        high_rows = rows + 8
        def layer(l, _):
            center = jnp.concatenate([src[l + 1, zt, 8 : 8 + high_rows, :] for zt in range(blocks)], axis=0)
            high = center.astype(BF16)
            low = (center - high.astype(F32)).astype(BF16)
            both = dot_nn(jnp.concatenate([high, low], axis=1), weights[...])
            part = [both[zt * high_rows : (zt + 1) * high_rows, :] for zt in range(blocks)]
            nothing = jnp.zeros((high_rows, TILE), F32)
            left_lanes = lax.broadcasted_iota(I32, nothing.shape, 1) < TILE // 2
            for zt in range(blocks):
                end = jnp.where(left_lanes, part[zt - 1][:, TILE:] if zt > 0 else nothing,
                                part[zt + 1][:, TILE:] if zt + 1 < blocks else nothing)
                beside = src[l, zt, 8 : 8 + high_rows, :] + src[l + 2, zt, 8 : 8 + high_rows, :]
                beside = beside + (src[l + 1, zt, 7 : 7 + high_rows, :] + src[l + 1, zt, 9 : 9 + high_rows, :])
                beside = beside + (part[zt][:, :TILE] + end)
                value = src[l + 1, zt, 8 : 8 + high_rows, :] + wide_coefs[l, zt, 4 : 4 + high_rows, :] * beside
                dst[l + 1, zt, 8 : 8 + high_rows, :] = value
            return 0

        lax.fori_loop(0, layers_now, layer, 0)
        for zt in range(blocks):
            dst[1, zt, 8 : 8 + high_rows, :] += wide_source[zt, 4 : 4 + high_rows, :]

    owners[...] = onehot(devices, row_of(owner))
    slots[...] = onehot(SLOTS, ranks(owners[...], devices).astype(I32), F32)

    for copy in near:
        copy.wait_recv()
    put_features(near_pos[...], row_of(near_temp), left, None)
    for t in range(tiles):
        put_tile(left, t, tiles + t, lefts, across)

    none = jnp.zeros((32, TILE), BF16)

    def pair_group(group, _):
        for k in range(0, UNROLL, 2):
            number = group * UNROLL + k
            first = [codes[0, number + n] & (tiles - 1) for n in (0, 1)]
            second = [codes[1, number + n] & (2 * tiles - 1) for n in (0, 1)]
            stacked = jnp.concatenate([
                jnp.concatenate([rights[first[0]], none], axis=1),
                jnp.concatenate([none, rights[first[1]]], axis=1)], axis=0)
            both = dot_nn(lefts[0, second[0], :, 0:64] + lefts[1, second[1], :, 0:64], stacked)
            for n in (0, 1):
                close = jnp.maximum(both[:, n * TILE : (n + 1) * TILE], 0.0)
                gained = (close * close) * (across[second[n]] - own_temp[pl.ds(first[n], 1), :])
                at = pl.multiple_of((number + n) * 8, 8)
                partial[pl.ds(at, 8), :] = jnp.sum(gained.reshape(TILE // 8, 8, TILE), axis=0)
        return 0

    pairs = codes.shape[1]
    lax.fori_loop(0, pairs // UNROLL // 2, pair_group, 0)
    step(0)
    lax.fori_loop(pairs // UNROLL // 2, pairs // UNROLL, pair_group, 0)
    step(1)
    summed = partial[pl.ds(0, pairs, stride=8), :]
    for s in range(1, 8):
        summed = summed + partial[pl.ds(s, pairs, stride=8), :]
    code_row = code_rows[0:1, :]
    number = lax.broadcasted_iota(I32, code_row.shape, 1)
    first = jnp.where(number < count[0], code_row & (tiles - 1), -1)
    firsts = onehot(tiles, first)
    gain = jnp.zeros((tiles, TILE), F32)
    for part in split3(summed):
        gain = gain + dot_nn(firsts, part.astype(BF16))
    out_temp = own_temp[...] + HEAT_RATE * gain
    heated[...] = out_temp

    parts = jnp.concatenate(split3(out_temp), axis=0).T.astype(BF16)
    which_row = row_of(which)
    high = onehot(tiles, lax.shift_right_logical(which_row, 7))
    picked = dot_nn(parts, jnp.concatenate([high] * 3, axis=0))
    low = jnp.broadcast_to(which_row & (TILE - 1), picked.shape)
    hit = lax.broadcasted_iota(I32, picked.shape, 0) == low
    flux = WALL_HEAT * (jnp.sum(jnp.where(hit, picked, 0.0), axis=0, keepdims=True) - row_of(seen))
    slot = slots[...]
    cell_row = row_of(cell)
    cells = ((cell_row & ~255).astype(F32), (cell_row & 255).astype(F32), None)
    total = jnp.zeros((devices, 2 * SLOTS), F32)
    for f, c in zip(split3(flux), cells):
        lower_half = jnp.zeros_like(slot) if c is None else slot * c
        total = total + dot_nt(owners[...], jnp.concatenate([slot * f, lower_half], axis=0).astype(BF16))
    send[...] = jnp.concatenate([total, jnp.zeros((devices, TILE - 2 * SLOTS), F32)], axis=1)

    def spread_out(src, dst, sends, recvs):
        everyone(lambda f, s: pltpu.make_async_remote_copy(
            src_ref=src.at[pl.ds(f * subs + s, 1)], dst_ref=dst.at[pl.ds(me, 1)], send_sem=sends, recv_sem=recvs,
            device_id=(f, s), device_id_type=MESH).start())
        return pltpu.make_async_remote_copy(
            src_ref=src.at[pl.ds(0, devices - 1)], dst_ref=dst.at[pl.ds(0, devices - 1)], send_sem=sends,
            recv_sem=recvs, device_id=behind, device_id_type=MESH)

    own = pltpu.make_async_copy(send.at[pl.ds(me, 1)], recv.at[pl.ds(me, 1)], own_sem.at[0])
    own.start()
    first_trip = spread_out(send, recv, first_send, first_recv)

    step(2)

    own.wait()
    first_trip.wait_recv()
    turned[...] = recv[...].T

    def place_slot(n, _):
        for k in range(4):
            s = n * 4 + k
            code = turned[pl.ds(SLOTS + s, 1), :].astype(I32)
            flux = turned[pl.ds(s, 1), :] * (1.0 / SUBSTEPS)
            at = pl.ds(pl.multiple_of(s * devices, TILE), devices)
            hot[:, at] = onehot(hot.shape[0], plate_row(code))
            low = onehot(TILE, code & (TILE - 1), F32)
            for m, part in enumerate(split2(flux)):
                lows[m * TILE : (m + 1) * TILE, at] = (low * part).astype(BF16)
        return 0

    lax.fori_loop(0, SLOTS // 4, place_slot, 0, unroll=2)
    total = dot_nt(hot[...], lows[...])
    total = total[:, :TILE] + total[:, TILE:]
    for zt in range(blocks):
        source[zt] = total[zt * rows : (zt + 1) * rows, :]
        wide_source[zt, 8 : 8 + rows, :] = total[zt * rows : (zt + 1) * rows, :]
    each(lambda side: side_copy(1, side).start())
    step(3)
    ahead = 2
    step(4, 0, ahead)

    for n in (0, 1):
        each(lambda side: side_copy(n, 1 - side).wait_recv())
    for zt in range(blocks):
        resp[1, zt, 8 : 16 + rows, :] = wide_source[zt, 4 : 12 + rows, :]
        resp[1, zt, 7:8, :] = wide_source[zt, 3:4, :]
        resp[1, zt, 16 + rows : 17 + rows, :] = wide_source[zt, 12 + rows : 13 + rows, :]

    def respond_twice(n, _):
        respond(resp, resp_next, 2 * n)
        respond(resp_next, resp, 2 * n + 1)
        return 0

    lax.fori_loop(1, EARLY // 2 + 1, respond_twice, 0)
    done = resp
    target = (cur, nxt)[EARLY % 2]
    for c in range(ahead):
        arrive(EARLY, c)
        drain(EARLY, c)
    for l in range(EARLY):
        for zt in range(blocks):
            target[l + 1, zt, TOP : TOP + rows, :] += done[l + 1, zt, 12 : 12 + rows, :]
            target[l + 1, zt, LOW : LOW + 1, :] += done[l + 1, zt, 11:12, :]
            target[l + 1, zt, TOP + rows : TOP + rows + 1, :] += done[l + 1, zt, 12 + rows : 13 + rows, :]

    last = SUBSTEPS - 1
    advance(nxt, None, 0)
    for zt in range(blocks):
        out[0, :, zt * TILE : (zt + 1) * TILE] += source[zt]
    flat = jnp.concatenate([out[0, :, zt * TILE : (zt + 1) * TILE] for zt in range(blocks)], axis=0)
    wide = jnp.concatenate([flat[k : k + TILE, :].T for k in range(0, flat.shape[0], TILE)], axis=1)
    parts = jnp.concatenate(split2(wide), axis=0).astype(BF16)

    def pick_slots(n, _):
        for k in range(2):
            at = pl.ds(pl.multiple_of((n * 2 + k) * 2 * devices, TILE), 2 * devices)
            found = dot_nn(parts, hot[:, at])
            found = found[:TILE] + found[TILE:]
            s = n * 4 + k * 2
            code = jnp.concatenate([turned[pl.ds(SLOTS + s + m, 1), :] for m in (0, 1)], axis=1).astype(I32)
            low = lax.broadcasted_iota(I32, found.shape, 0) == jnp.broadcast_to(code & (TILE - 1), found.shape)
            value = jnp.sum(jnp.where(low, found, 0.0), axis=0, keepdims=True)
            for m in (0, 1):
                found_rows[pl.ds(s + m, 1), :] = value[:, m * devices : (m + 1) * devices]
        return 0

    found_rows[...] = jnp.zeros(found_rows.shape, F32)
    lax.fori_loop(0, SLOTS // 4, pick_slots, 0, unroll=2)
    values[...] = found_rows[...].T
    own = pltpu.make_async_copy(values.at[pl.ds(me, 1)], back.at[pl.ds(me, 1)], own_sem.at[1])
    own.start()
    last_trip = spread_out(values, back, last_send, last_recv)
    step(4, ahead, CHUNKS)

    def closing(c, _):
        pl.when(c >= ahead)(lambda: arrive(last, c))
        advance(nxt, None, c)
        return 0

    lax.fori_loop(1, CHUNKS, closing, 0)

    own.wait()
    last_trip.wait_recv()
    found = dot_nn(jnp.concatenate(split2(back[...].T[0:SLOTS, :]), axis=0).astype(BF16), owners[...])
    ghost = jnp.sum((found[0:SLOTS] + found[SLOTS:]) * slots[...], axis=0, keepdims=True)
    for t in range(ghost_out.shape[0]):
        ghost_out[t : t + 1, :] = ghost[:, t * TILE : (t + 1) * TILE]

    for copy in near:
        copy.wait_send()
    first_trip.wait_send()
    last_trip.wait_send()
    for c in range(CHUNKS):
        drain(last - 1, c)
        if c >= ahead:
            drain(last, c)
    for n in (0, 1):
        each(lambda side: side_copy(n, side).wait_send())


def call_step(codes, count, own_pos, own_temp, which, owner, cell, seen, temp, coef, fluids, subs):
    devices = fluids * subs
    layers, rows, span = temp.shape
    blocks = span // TILE
    tiles, wide = own_temp.shape[0], own_pos.shape[1]
    ghosts = owner.shape[0] * TILE
    DMA = pltpu.SemaphoreType.DMA
    return pl.pallas_call(
        functools.partial(step_kernel, fluids, subs),
        out_shape=(
            pltpu.VMEM(own_temp.shape, F32),
            pltpu.VMEM(temp.shape, F32),
            pltpu.VMEM(owner.shape, F32),
        ),
        in_specs=[SMEM_SPEC] + [HBM_SPEC] * 9,
        out_specs=(VMEM_SPEC,) * 3,
        scratch_shapes=[
            pltpu.SMEM(codes.shape, I32),
            pltpu.VMEM(codes.shape, I32),
            pltpu.VMEM(own_pos.shape, F32),
            pltpu.VMEM(own_temp.shape, F32),
            pltpu.VMEM(which.shape, I32),
            pltpu.VMEM(owner.shape, I32),
            pltpu.VMEM(cell.shape, I32),
            pltpu.VMEM(seen.shape, F32),
            DMA((8,)),
            pltpu.VMEM((32, wide), F32),
            pltpu.VMEM((32, wide), F32),
            pltpu.VMEM((2, 2 * tiles, TILE, TILE), BF16),
            pltpu.VMEM((2 * tiles, TILE, TILE), F32),
            pltpu.VMEM((tiles, 32, TILE), BF16),
            pltpu.VMEM((codes.shape[1] * 8, TILE), F32),
            pltpu.VMEM(own_pos.shape, F32),
            pltpu.VMEM(own_temp.shape, F32),
            pltpu.VMEM((devices, ghosts), BF16),
            pltpu.VMEM((SLOTS, ghosts), F32),
            pltpu.VMEM((devices, TILE), F32),
            pltpu.VMEM((devices, TILE), F32),
            pltpu.VMEM((TILE, devices), F32),
            pltpu.VMEM((TILE, devices), F32),
            pltpu.VMEM((rows * blocks, devices * SLOTS), BF16),
            pltpu.VMEM((2 * TILE, devices * SLOTS), BF16),
            pltpu.VMEM((blocks, rows, TILE), F32),
            pltpu.VMEM((devices, TILE), F32),
            pltpu.VMEM((devices, TILE), F32),
            pltpu.VMEM((layers + 2, blocks, TOP + rows + 8, TILE), F32),
            pltpu.VMEM((layers + 2, blocks, TOP + rows + 8, TILE), F32),
            pltpu.VMEM((layers, blocks, rows, TILE), F32),
            pltpu.VMEM((2 * TILE, 2 * TILE), BF16),
            pltpu.VMEM((blocks, rows + 16, TILE), F32),
            pltpu.VMEM((EARLY, blocks, rows + 16, TILE), F32),
            pltpu.VMEM((EARLY + 2, blocks, rows + 32, TILE), F32),
            pltpu.VMEM((EARLY + 2, blocks, rows + 32, TILE), F32),
            DMA((2, 2)),
            DMA((2, 2)),
            DMA((2,)),
            DMA((2,)),
            DMA,
            DMA,
            DMA,
            DMA,
            DMA((2,)),
            DMA((2, blocks)),
            DMA((SUBSTEPS, 2, CHUNKS)),
            DMA((SUBSTEPS, 2, CHUNKS)),
        ],
        compiler_params=pltpu.CompilerParams(collective_id=0, has_side_effects=True, vmem_limit_bytes=48 << 20),
        name="step",
    )(count, *[pltpu.with_memory_space_constraint(x, pltpu.HBM) for x in (
        codes, own_pos, own_temp, which, owner, cell, seen, temp, coef)])


def finish_kernel(plate, first, second, plate_out, first_out, second_out, sem):
    deep = plate.shape[0] // 8
    copies = [pltpu.make_async_copy(plate.at[pl.ds(n * deep, deep)], plate_out.at[pl.ds(n * deep, deep)], sem.at[n]) for n in range(8)]
    copies.append(pltpu.make_async_copy(first, first_out, sem.at[8]))
    copies.append(pltpu.make_async_copy(second, second_out, sem.at[9]))
    for copy in copies:
        copy.start()
    for copy in copies:
        copy.wait()


def call_finish(*arrays):
    return pl.pallas_call(
        finish_kernel,
        out_shape=tuple(jax.ShapeDtypeStruct(x.shape, x.dtype) for x in arrays),
        in_specs=[VMEM_SPEC] * 3,
        out_specs=(HBM_SPEC,) * 3,
        scratch_shapes=[pltpu.SemaphoreType.DMA((10,))],
        compiler_params=pltpu.CompilerParams(vmem_limit_bytes=16 << 20),
        name="finish",
    )(*arrays)


def on_device(positions, particle_temp, pair_list, pair_count, ghost_particle, ghost_owner, ghost_cell,
              wall_seen, solid_temp, conduct):
    codes = pair_list.T

    def tiled(x):
        return x.reshape(-1, TILE)

    heated, temp, ghost = call_step(
        codes, pair_count, positions, tiled(particle_temp), tiled(ghost_particle), tiled(ghost_owner),
        tiled(ghost_cell), tiled(wall_seen), solid_temp, conduct, lax.axis_size(AXES[0]), lax.axis_size(AXES[1]))
    temp, heated, ghost = call_finish(temp, heated, ghost)
    return heated.reshape(-1), temp, ghost.reshape(-1)


def solution(mesh):
    one, rows, plate = P(AXES), P(AXES, None), P(None, AXES, None)
    return jax.shard_map(
        on_device,
        mesh=mesh,
        in_specs=(P(None, AXES), one, rows, one, one, rows, one, one, plate, plate),
        out_specs=(one, plate, one),
        check_vma=False,
    )
```
